32 devices in a mesh: row: 8 (over y, x, core), col: 4 (over z).
Axes of the slice: x: 2, y: 2, z: 4, core: 2. Of those that a mesh axis runs over, the one named last changes fastest.
Arguments:
- p_cov: bfloat16 [4096, 4096], P('row', 'col'), may hold values from -6 to 6, as said below
- f_blocks: bfloat16 [32, 7, 128, 128], P('row'), may hold values from -0.1875 to 0.1875
- stencil_cols: int32 [32, 7], replicated, may hold values from 0 to 31, as said below
- localization_weights: bfloat16 [4096, 4096], P('row', 'col'), may hold values from 0.25 to 1, as said below
- block_mask: int32 [32, 32], P('row', 'col'), may hold values from 0 to 1, as said below
- disturbance_variances: float32 [4096], P('row'), may hold values from 0.5 to 2
Outputs:
- predicted_spread_matrix: float32 [4096, 4096], P('row', 'col')
The draws below stay inside these ranges and needn't reach their ends.
Inputs may be any that keep to these rules, and one draw needn't show every extreme that they name: `stencil_cols`: block row i lists i, i - 1, i + 1, one block 2 to 3 above and one below, and i - 4 and i + 4, each clamped to 0 .. 31. Symmetric: p_cov equals its transpose. `localization_weights`: Symmetric: taper equals its transpose. Symmetric: block_mask equals its transpose.
All inputs are finite; a program needn't handle non-finite values.
Results may differ from the reference program's by a relative error of at most 0.0029.
Values may be sent and summed in bfloat16 or wider, within the bound.
No kernel may reach another device: no remote copies, remote signals or barrier semaphores. Data moves between devices by JAX's collectives and lax.ppermute only.
A program may use at most 64 MiB of HBM per device.

```python
import math
import jax
import jax.numpy as jnp

BS = 128
STENCIL = 7
BAND = 4
NB = 32
STATE_DIMENSION = 4096


def draw_stencil_cols(key, part):
    first_key, second_key = jax.random.split(jax.random.fold_in(key, 17))
    base = jnp.arange(NB, dtype=jnp.int32)
    upper = jax.random.randint(first_key, (NB,), 2, BAND, dtype=jnp.int32)
    lower = jax.random.randint(second_key, (NB,), 2, BAND, dtype=jnp.int32)
    zeros = jnp.zeros((NB,), jnp.int32)
    ones = jnp.ones((NB,), jnp.int32)
    reach = jnp.full((NB,), BAND, jnp.int32)
    offsets = jnp.stack([zeros, ones, -ones, upper, -lower, reach, -reach], axis=1)
    return jnp.clip(base[:, None] + offsets, 0, NB - 1).astype(jnp.int32)


def draw_p_cov(key, part):
    first_key = jax.random.fold_in(jax.random.fold_in(key, 29), 0)
    raw = jax.random.normal(first_key, (STATE_DIMENSION, STATE_DIMENSION), jnp.float32)
    sym = (raw + raw.T) * 0.70710678
    return jnp.clip(sym, -6.0, 6.0).astype(jnp.bfloat16)


def draw_localization_weights(key, part):
    raw = jax.random.uniform(jax.random.fold_in(key, 31), (STATE_DIMENSION, STATE_DIMENSION), jnp.float32, 0.0, 1.0)
    values = 0.25 + 0.75 * raw
    lower = jnp.tril(values)
    sym = lower + jnp.tril(values, -1).T
    return sym.astype(jnp.bfloat16)


def draw_block_mask(key, part):
    raw = jax.random.randint(jax.random.fold_in(key, 37), (NB, NB), 0, 4, dtype=jnp.int32)
    kept = (raw > 0).astype(jnp.int32)
    lower = jnp.tril(kept)
    return (lower + jnp.tril(kept, -1).T).astype(jnp.int32)


def shard_levels(key, dims, pieces, low, largest):
    def one(axis_at, shards_of):
        heights = jax.random.uniform(jax.random.fold_in(jax.random.fold_in(key, 6), axis_at), (shards_of,), jnp.float32, low / len(pieces), largest / len(pieces))
        return jnp.repeat(jnp.exp(heights), dims[axis_at] // shards_of).reshape((-1,) + (1,) * (len(dims) - axis_at - 1))

    loudness = one(*pieces[0])
    for cut in pieces[1:]:
        loudness = loudness * one(*cut)
    return loudness


def scatter_about(stream_key, extent, width, most, shards=(), kind=jnp.bfloat16):
    values = jax.random.normal(stream_key, extent, jnp.float32) * width
    if len(shards) > 0:
        values = shard_levels(stream_key, extent, shards, -0.22, 0.18) * values
    return jnp.clip(values, min=-most, max=most).astype(kind)


def setup_inputs(seed: int = 0) -> dict:
    streams_of = jax.random.split(jax.random.key(seed), 7)
    p_cov = draw_p_cov(jax.random.fold_in(streams_of[6], 71), 0)
    f_blocks = scatter_about(streams_of[1], (NB, STENCIL, BS, BS), (STENCIL * BS) ** -0.5, 0.1875, ((0, 8),))
    stencil_cols = draw_stencil_cols(jax.random.fold_in(streams_of[6], 71), 0)
    localization_weights = draw_localization_weights(jax.random.fold_in(streams_of[6], 71), 0)
    block_mask = draw_block_mask(jax.random.fold_in(streams_of[6], 71), 0)
    disturbance_variances = jnp.clip(jnp.exp(math.log(2.0) - 1.3862944 * jax.random.uniform(streams_of[5], (STATE_DIMENSION,), jnp.float32) ** shard_levels(streams_of[5], (STATE_DIMENSION,), ((0, 8),), -0.2, 0.2)), 0.5, 2.0)
    return {"p_cov": p_cov, "f_blocks": f_blocks, "stencil_cols": stencil_cols, "localization_weights": localization_weights, "block_mask": block_mask, "disturbance_variances": disturbance_variances}


def reference(p_cov, f_blocks, stencil_cols, localization_weights, block_mask, disturbance_variances):
    covariance_rows = p_cov.reshape(NB, BS, STATE_DIMENSION)
    inter = jnp.zeros((NB, BS, STATE_DIMENSION), jnp.float32)
    for entry in range(STENCIL):
        picked = covariance_rows[stencil_cols[:, entry]].astype(jnp.float32)
        inter = inter + jnp.einsum("iab,ibn->ian", f_blocks[:, entry].astype(jnp.float32), picked)
    inter = inter.reshape(STATE_DIMENSION, STATE_DIMENSION).astype(jnp.bfloat16)
    inter_cols = inter.reshape(STATE_DIMENSION, NB, BS)
    spread = jnp.zeros((STATE_DIMENSION, NB, BS), jnp.float32)
    for entry in range(STENCIL):
        picked = inter_cols[:, stencil_cols[:, entry], :].astype(jnp.float32)
        spread = spread + jnp.einsum("rjb,jab->rja", picked, f_blocks[:, entry].astype(jnp.float32))
    filtered_tile_entries = spread.reshape(NB, BS, NB, BS) * block_mask.astype(jnp.float32)[:, None, :, None]
    predicted_spread_matrix = localization_weights.astype(jnp.float32) * filtered_tile_entries.reshape(STATE_DIMENSION, STATE_DIMENSION)
    main_slot_position = jnp.arange(STATE_DIMENSION, dtype=jnp.int32)
    return predicted_spread_matrix.at[main_slot_position, main_slot_position].add(disturbance_variances)
```

```python
import functools

import jax
import jax.numpy as jnp
from jax import lax
from jax.experimental import pallas as pl
from jax.experimental.pallas import tpu as pltpu
from jax.sharding import PartitionSpec as P

STENCIL = 7
BAND = 4
ANY = pl.ANY


def up_down(devices):
    up = [(i, i + 1) for i in range(devices - 1)]
    return up, [(j, i) for i, j in up]


def source_plane(c, a, cols):
    if cols & (cols - 1):
        return a
    return c ^ (((a ^ c) - 1) % cols)


def group_pairs(rows, cols):
    fan = rows // cols
    pairs = []
    for t in range(rows):
        a, k = divmod(t, fan)
        for c in range(cols):
            if a != c:
                pairs.append(((c * fan + k) * cols + source_plane(c, a, cols), t * cols + c))
    return pairs


def stage1_kernel(cols_ref, f_ref, before_hbm, own_hbm, after_hbm, out_ref, ext, sem):
    rows = f_ref.shape[0]
    bs = f_ref.shape[2]
    n = out_ref.shape[1]
    first = lax.axis_index("row") * rows
    halo = before_hbm.shape[0]
    tall = own_hbm.shape[0]
    copies = [
        pltpu.make_async_copy(own_hbm, ext.at[pl.ds(halo, tall)], sem.at[0]),
        pltpu.make_async_copy(before_hbm, ext.at[pl.ds(0, halo)], sem.at[1]),
        pltpu.make_async_copy(after_hbm, ext.at[pl.ds(halo + tall, halo)], sem.at[2]),
    ]
    for copy in copies:
        copy.start()
    for copy in copies:
        copy.wait()
    tile = min(256, n)
    for i in range(rows):
        lhs = jnp.concatenate([f_ref[i, e] for e in range(STENCIL)], axis=1)
        starts = [
            pl.multiple_of((cols_ref[first + i, e] - first + BAND) * bs, bs)
            for e in range(STENCIL)
        ]
        for t in range(n // tile):
            rhs = jnp.concatenate(
                [ext[pl.ds(s, bs), t * tile : (t + 1) * tile] for s in starts], axis=0
            )
            out_ref[i * bs : (i + 1) * bs, t * tile : (t + 1) * tile] = jnp.dot(
                lhs, rhs, preferred_element_type=jnp.float32
            ).astype(out_ref.dtype)


def stage2_kernel(
    fan, cols_ref, mask_ref, q_ref, w_ref, left_hbm, own_hbm, right_hbm, mine_hbm, others_hbm,
    out_ref, ext, f_all, sem,
):
    j = pl.program_id(0)
    slab = pl.num_programs(0)
    bs = out_ref.shape[1]
    rows = out_ref.shape[0] // bs
    group = f_all.shape[0] // fan
    row_idx, col_idx = lax.axis_index("row"), lax.axis_index("col")
    halo, wide = left_hbm.shape[1], own_hbm.shape[1]

    @pl.when(j == 0)
    def _():
        k = lax.rem(row_idx, fan)
        copies = [
            pltpu.make_async_copy(own_hbm, ext.at[:, pl.ds(halo, wide)], sem.at[0]),
            pltpu.make_async_copy(left_hbm, ext.at[:, pl.ds(0, halo)], sem.at[1]),
            pltpu.make_async_copy(right_hbm, ext.at[:, pl.ds(halo + wide, halo)], sem.at[2]),
            pltpu.make_async_copy(mine_hbm, f_all.at[pl.ds(k * group, group)], sem.at[3]),
        ]
        for step in range(1, fan):
            at = lax.rem(k + step, fan) * group
            copies.append(
                pltpu.make_async_copy(
                    others_hbm.at[step - 1], f_all.at[pl.ds(at, group)], sem.at[3 + step]
                )
            )
        for copy in copies:
            copy.start()
        for copy in copies:
            copy.wait()

    col = col_idx * slab + j
    first = col_idx * slab - BAND
    lhs = jnp.concatenate(
        [
            ext[:, pl.ds(pl.multiple_of((cols_ref[col, e] - first) * bs, bs), bs)]
            for e in range(STENCIL)
        ],
        axis=1,
    )
    rhs = jnp.concatenate([f_all[j, e] for e in range(STENCIL)], axis=1)
    spread = lax.dot_general(
        lhs, rhs, (((1,), (1,)), ((), ())), preferred_element_type=jnp.float32
    )
    eye = lax.broadcasted_iota(jnp.int32, (bs, bs), 0) == lax.broadcasted_iota(
        jnp.int32, (bs, bs), 1
    )
    for i in range(rows):
        at = slice(i * bs, (i + 1) * bs)
        keep = mask_ref[i, j].astype(jnp.float32)
        on_main = (row_idx * rows + i == col).astype(jnp.float32)
        noise = jnp.where(eye, q_ref[i : i + 1, :] * on_main, 0.0)
        out_ref[at, :] = w_ref[at, :].astype(jnp.float32) * (spread[at] * keep) + noise


def on_device(
    p_cov, f_blocks, stencil_cols, localization_weights, block_mask, disturbance_variances
):
    rows, cols = lax.axis_size("row"), lax.axis_size("col")
    fan = rows // cols
    block_rows, bs = f_blocks.shape[0], f_blocks.shape[2]
    tall, wide = p_cov.shape
    slab = wide // bs
    halo = BAND * bs

    up, down = up_down(rows)
    before = lax.ppermute(p_cov[tall - halo :], "row", up)
    after = lax.ppermute(p_cov[:halo], "row", down)
    mine = jnp.where(
        lax.axis_index("row") // fan == lax.axis_index("col"),
        f_blocks,
        lax.ppermute(f_blocks, ("row", "col"), group_pairs(rows, cols)),
    )
    others = []
    for step in range(1, fan):
        turn = [(r // fan * fan + (r + step) % fan, r) for r in range(rows)]
        others.append(lax.ppermute(mine, "row", turn))
    others = jnp.stack(others)

    smem = pl.BlockSpec(memory_space=pltpu.SMEM)
    hbm = pl.BlockSpec(memory_space=ANY)
    vmem = pl.BlockSpec(memory_space=pltpu.VMEM)
    inter = pl.pallas_call(
        stage1_kernel,
        out_shape=jax.ShapeDtypeStruct((tall, wide), jnp.bfloat16),
        in_specs=[smem, vmem, hbm, hbm, hbm],
        out_specs=vmem,
        scratch_shapes=[
            pltpu.VMEM((tall + 2 * halo, wide), jnp.bfloat16),
            pltpu.SemaphoreType.DMA((3,)),
        ],
        compiler_params=pltpu.CompilerParams(vmem_limit_bytes=16 * 2**20),
        name="stage1",
    )(stencil_cols, f_blocks, before, p_cov, after)

    up, down = up_down(cols)
    left = lax.ppermute(inter[:, wide - halo :], "col", up)
    right = lax.ppermute(inter[:, :halo], "col", down)

    return pl.pallas_call(
        functools.partial(stage2_kernel, fan),
        out_shape=jax.ShapeDtypeStruct((tall, wide), jnp.float32),
        grid=(slab,),
        in_specs=[
            smem,
            smem,
            pl.BlockSpec((block_rows, bs), lambda j: (0, 0)),
            pl.BlockSpec((tall, bs), lambda j: (0, j)),
            hbm,
            hbm,
            hbm,
            hbm,
            hbm,
        ],
        out_specs=pl.BlockSpec((tall, bs), lambda j: (0, j)),
        scratch_shapes=[
            pltpu.VMEM((tall, wide + 2 * halo), jnp.bfloat16),
            pltpu.VMEM((slab, STENCIL, bs, bs), jnp.bfloat16),
            pltpu.SemaphoreType.DMA((3 + fan,)),
        ],
        compiler_params=pltpu.CompilerParams(vmem_limit_bytes=16 * 2**20),
        name="stage2",
    )(
        stencil_cols,
        block_mask,
        disturbance_variances.reshape(block_rows, bs),
        localization_weights,
        left,
        inter,
        right,
        mine,
        others,
    )


def solution(mesh):
    placed = (
        P("row", "col"),
        P("row", None, None, None),
        P(),
        P("row", "col"),
        P("row", "col"),
        P("row"),
    )
    return jax.shard_map(
        on_device, mesh=mesh, in_specs=placed, out_specs=P("row", "col"), check_vma=False
    )
```

```python
import functools

import jax
import jax.numpy as jnp
from jax import lax
from jax.experimental import pallas as pl
from jax.experimental.pallas import tpu as pltpu
from jax.sharding import PartitionSpec as P


STENCIL = 7
BAND = 4
ANY = pl.ANY


def up_down(devices):
    up = [(i, i + 1) for i in range(devices - 1)]
    return up, [(j, i) for i, j in up]


def source_plane(c, a, cols):
    if cols & (cols - 1):
        return a
    return c ^ (((a ^ c) - 1) % cols)


def group_steps(rows, cols):
    fan = rows // cols

    def at(a, k, c):
        return (a * fan + k) * cols + c

    if (cols, fan) != (4, 2):
        pairs = []
        for c in range(cols):
            for a in range(cols):
                if a != c:
                    plane = source_plane(c, a, cols)
                    pairs += [(at(c, k, plane), at(a, k, c)) for k in range(fan)]
        return [pairs]
    first, second = [], []
    for c in range(cols):
        near, side, far, plane = c ^ 1, c ^ 2, c ^ 3, c ^ 3
        first += [
            (at(c, 0, c), at(near, 0, c)),
            (at(c, 1, c), at(side, 1, c)),
            (at(c, 1, plane), at(near, 0, plane)),
            (at(c, 0, plane), at(side, 1, plane)),
        ]
        second += [
            (at(near, 0, c), at(far, 0, c)),
            (at(side, 1, c), at(far, 1, c)),
            (at(near, 0, plane), at(near, 1, c)),
            (at(side, 1, plane), at(side, 0, c)),
        ]
    return [first, second]


def holder_table(rows, cols):
    table = [0] * (rows * cols)
    for step, pairs in enumerate(group_steps(rows, cols)):
        for _, target in pairs:
            table[target] = step + 1
    for a in range(cols):
        for k in range(rows // cols):
            table[(a * (rows // cols) + k) * cols + a] = 0
    return table


def pick_kernel(table, *refs):
    *sources, out_ref, sem = refs
    me = lax.axis_index("row") * lax.axis_size("col") + lax.axis_index("col")
    which = 0
    for device, step in enumerate(table):
        if step:
            which = jnp.where(me == device, step, which)
    for step, source in enumerate(sources):

        @pl.when(which == step)
        def _():
            copy = pltpu.make_async_copy(source, out_ref, sem)
            copy.start()
            copy.wait()


def stage1_kernel(cols_ref, f_ref, before_hbm, own_hbm, after_hbm, out_ref, ext, sem):
    rows = f_ref.shape[0]
    bs = f_ref.shape[2]
    n = out_ref.shape[1]
    first = lax.axis_index("row") * rows
    halo = before_hbm.shape[0]
    tall = own_hbm.shape[0]
    copies = [
        pltpu.make_async_copy(own_hbm, ext.at[pl.ds(halo, tall)], sem.at[0]),
        pltpu.make_async_copy(before_hbm, ext.at[pl.ds(0, halo)], sem.at[1]),
        pltpu.make_async_copy(after_hbm, ext.at[pl.ds(halo + tall, halo)], sem.at[2]),
    ]
    for copy in copies:
        copy.start()
    for copy in copies:
        copy.wait()
    tile = min(256, n)
    for i in range(rows):
        lhs = jnp.concatenate([f_ref[i, e] for e in range(STENCIL)], axis=1)
        starts = [
            pl.multiple_of((cols_ref[first + i, e] - first + BAND) * bs, bs)
            for e in range(STENCIL)
        ]
        for t in range(n // tile):
            rhs = jnp.concatenate(
                [ext[pl.ds(s, bs), t * tile : (t + 1) * tile] for s in starts], axis=0
            )
            out_ref[i * bs : (i + 1) * bs, t * tile : (t + 1) * tile] = jnp.dot(
                lhs, rhs, preferred_element_type=jnp.float32
            ).astype(out_ref.dtype)


def stage2_kernel(
    fan, cols_ref, mask_ref, q_ref, w_ref, left_hbm, own_hbm, right_hbm, mine_hbm, others_hbm,
    out_ref, ext, f_all, sem,
):
    j = pl.program_id(0)
    slab = pl.num_programs(0)
    bs = out_ref.shape[1]
    rows = out_ref.shape[0] // bs
    group = f_all.shape[0] // fan
    row_idx, col_idx = lax.axis_index("row"), lax.axis_index("col")
    halo, wide = left_hbm.shape[1], own_hbm.shape[1]

    @pl.when(j == 0)
    def _():
        k = lax.rem(row_idx, fan)
        copies = [
            pltpu.make_async_copy(own_hbm, ext.at[:, pl.ds(halo, wide)], sem.at[0]),
            pltpu.make_async_copy(left_hbm, ext.at[:, pl.ds(0, halo)], sem.at[1]),
            pltpu.make_async_copy(right_hbm, ext.at[:, pl.ds(halo + wide, halo)], sem.at[2]),
            pltpu.make_async_copy(mine_hbm, f_all.at[pl.ds(k * group, group)], sem.at[3]),
        ]
        for step in range(1, fan):
            at = lax.rem(k + step, fan) * group
            copies.append(
                pltpu.make_async_copy(
                    others_hbm.at[step - 1], f_all.at[pl.ds(at, group)], sem.at[3 + step]
                )
            )
        for copy in copies:
            copy.start()
        for copy in copies:
            copy.wait()

    col = col_idx * slab + j
    first = col_idx * slab - BAND
    lhs = jnp.concatenate(
        [
            ext[:, pl.ds(pl.multiple_of((cols_ref[col, e] - first) * bs, bs), bs)]
            for e in range(STENCIL)
        ],
        axis=1,
    )
    rhs = jnp.concatenate([f_all[j, e] for e in range(STENCIL)], axis=1)
    spread = lax.dot_general(
        lhs, rhs, (((1,), (1,)), ((), ())), preferred_element_type=jnp.float32
    )
    eye = lax.broadcasted_iota(jnp.int32, (bs, bs), 0) == lax.broadcasted_iota(
        jnp.int32, (bs, bs), 1
    )
    for i in range(rows):
        at = slice(i * bs, (i + 1) * bs)
        keep = mask_ref[i, j].astype(jnp.float32)
        on_main = (row_idx * rows + i == col).astype(jnp.float32)
        noise = jnp.where(eye, q_ref[i : i + 1, :] * on_main, 0.0)
        out_ref[at, :] = w_ref[at, :].astype(jnp.float32) * (spread[at] * keep) + noise


def forecast(
    p_cov, f_blocks, stencil_cols, localization_weights, block_mask, disturbance_variances
):
    rows, cols = lax.axis_size("row"), lax.axis_size("col")
    fan = rows // cols
    block_rows, bs = f_blocks.shape[0], f_blocks.shape[2]
    tall, wide = p_cov.shape
    slab = wide // bs
    halo = BAND * bs

    up, down = up_down(rows)
    before = lax.ppermute(p_cov[tall - halo :], "row", up)
    after = lax.ppermute(p_cov[:halo], "row", down)
    steps = group_steps(rows, cols)
    held = [f_blocks]
    for pairs in steps:
        held.append(lax.ppermute(held[-1], ("row", "col"), pairs))
    mine = pl.pallas_call(
        functools.partial(pick_kernel, holder_table(rows, cols)),
        out_shape=jax.ShapeDtypeStruct(f_blocks.shape, f_blocks.dtype),
        in_specs=[pl.BlockSpec(memory_space=ANY)] * len(held),
        out_specs=pl.BlockSpec(memory_space=pltpu.VMEM),
        scratch_shapes=[pltpu.SemaphoreType.DMA],
        compiler_params=pltpu.CompilerParams(vmem_limit_bytes=4 * 2**20),
        name="pick",
    )(*held)
    others = []
    for step in range(1, fan):
        turn = [(r // fan * fan + (r + step) % fan, r) for r in range(rows)]
        others.append(lax.ppermute(mine, "row", turn))
    others = jnp.stack(others)

    smem = pl.BlockSpec(memory_space=pltpu.SMEM)
    hbm = pl.BlockSpec(memory_space=ANY)
    vmem = pl.BlockSpec(memory_space=pltpu.VMEM)
    inter = pl.pallas_call(
        stage1_kernel,
        out_shape=jax.ShapeDtypeStruct((tall, wide), jnp.bfloat16),
        in_specs=[smem, vmem, hbm, hbm, hbm],
        out_specs=vmem,
        scratch_shapes=[
            pltpu.VMEM((tall + 2 * halo, wide), jnp.bfloat16),
            pltpu.SemaphoreType.DMA((3,)),
        ],
        compiler_params=pltpu.CompilerParams(vmem_limit_bytes=16 * 2**20),
        name="stage1",
    )(stencil_cols, f_blocks, before, p_cov, after)

    up, down = up_down(cols)
    left = lax.ppermute(inter[:, wide - halo :], "col", up)
    right = lax.ppermute(inter[:, :halo], "col", down)

    return pl.pallas_call(
        functools.partial(stage2_kernel, fan),
        out_shape=jax.ShapeDtypeStruct((tall, wide), jnp.float32),
        grid=(slab,),
        in_specs=[
            smem,
            smem,
            pl.BlockSpec((block_rows, bs), lambda j: (0, 0)),
            pl.BlockSpec((tall, bs), lambda j: (0, j)),
            hbm,
            hbm,
            hbm,
            hbm,
            hbm,
        ],
        out_specs=pl.BlockSpec((tall, bs), lambda j: (0, j)),
        scratch_shapes=[
            pltpu.VMEM((tall, wide + 2 * halo), jnp.bfloat16),
            pltpu.VMEM((slab, STENCIL, bs, bs), jnp.bfloat16),
            pltpu.SemaphoreType.DMA((3 + fan,)),
        ],
        compiler_params=pltpu.CompilerParams(vmem_limit_bytes=16 * 2**20),
        name="stage2",
    )(
        stencil_cols,
        block_mask,
        disturbance_variances.reshape(block_rows, bs),
        localization_weights,
        left,
        inter,
        right,
        mine,
        others,
    )


def solution(mesh):
    placed = (
        P("row", "col"),
        P("row", None, None, None),
        P(),
        P("row", "col"),
        P("row", "col"),
        P("row"),
    )
    return jax.shard_map(
        forecast, mesh=mesh, in_specs=placed, out_specs=P("row", "col"), check_vma=False
    )
```

```python
import functools

import jax
import jax.numpy as jnp
from jax import lax
from jax.experimental import pallas as pl
from jax.experimental.pallas import tpu as pltpu
from jax.sharding import PartitionSpec as P


STENCIL = 7
BAND = 4
ANY = pl.ANY


def up_down(devices):
    up = [(i, i + 1) for i in range(devices - 1)]
    return up, [(j, i) for i, j in up]


def source_plane(c, a, cols):
    if cols & (cols - 1):
        return a
    return c ^ (((a ^ c) - 1) % cols)


def group_plan(rows, cols):
    fan = rows // cols

    def at(a, k, c):
        return (a * fan + k) * cols + c

    if (cols, fan) != (4, 2):
        pairs = []
        for c in range(cols):
            for a in range(cols):
                if a != c:
                    plane = source_plane(c, a, cols)
                    pairs += [(at(c, k, plane), at(a, k, c)) for k in range(fan)]
        return [(0, pairs)]
    first, relayed, second = [], [], []
    for c in range(cols):
        near, side, far = c ^ 1, c ^ 2, c ^ 3
        first += [(at(c, 0, c), at(near, 0, c)), (at(c, 1, c), at(side, 1, c))]
        relayed += [(at(near, 0, c), at(far, 0, c)), (at(side, 1, c), at(far, 1, c))]
        second += [(at(c, 0, c), at(side, 0, c)), (at(c, 1, c), at(near, 1, c))]
    return [(0, first), (1, relayed), (0, second)]


def holder_table(rows, cols):
    table = [0] * (rows * cols)
    for step, (_, pairs) in enumerate(group_plan(rows, cols)):
        for _, target in pairs:
            table[target] = step + 1
    return table


def pick_kernel(table, *refs):
    *sources, out_ref, sem = refs
    me = lax.axis_index("row") * lax.axis_size("col") + lax.axis_index("col")
    which = 0
    for device, step in enumerate(table):
        if step:
            which = jnp.where(me == device, step, which)
    for step, source in enumerate(sources):

        @pl.when(which == step)
        def _():
            copy = pltpu.make_async_copy(source, out_ref, sem)
            copy.start()
            copy.wait()


def fetch_kernel(p_hbm, f_hbm, p_ref, f_ref, sem):
    copies = [
        pltpu.make_async_copy(p_hbm, p_ref, sem.at[0]),
        pltpu.make_async_copy(f_hbm, f_ref, sem.at[1]),
    ]
    for copy in copies:
        copy.start()
    for copy in copies:
        copy.wait()


def stage1_kernel(
    cols_ref, f_ref, before_hbm, own_hbm, after_hbm, low_ref, high_ref, ext, sem
):
    rows, bs = f_ref.shape[0], f_ref.shape[2]
    half = low_ref.shape[1]
    first = lax.axis_index("row") * rows
    halo, tall = before_hbm.shape[0], own_hbm.shape[0]
    copies = [
        pltpu.make_async_copy(before_hbm, ext.at[pl.ds(0, halo)], sem.at[0]),
        pltpu.make_async_copy(own_hbm, ext.at[pl.ds(halo, tall)], sem.at[1]),
        pltpu.make_async_copy(after_hbm, ext.at[pl.ds(halo + tall, halo)], sem.at[2]),
    ]
    for copy in copies:
        copy.start()
    for copy in copies:
        copy.wait()
    tile = min(256, half)
    for i in range(rows):
        lhs = jnp.concatenate([f_ref[i, e] for e in range(STENCIL)], axis=1)
        starts = [
            pl.multiple_of((cols_ref[e, first + i] - first + BAND) * bs, bs)
            for e in range(STENCIL)
        ]
        for part, out_ref in enumerate((low_ref, high_ref)):
            for t in range(half // tile):
                at = part * half + t * tile
                rhs = jnp.concatenate(
                    [ext[pl.ds(s, bs), at : at + tile] for s in starts], axis=0
                )
                out_ref[i * bs : (i + 1) * bs, t * tile : (t + 1) * tile] = jnp.dot(
                    lhs, rhs, preferred_element_type=jnp.float32
                ).astype(out_ref.dtype)


def stage2_kernel(
    fan, cols_ref, mask_ref, q_ref, w_ref, left_hbm, low_hbm, high_hbm, right_hbm, mine_hbm,
    others_hbm, out_ref, ext, f_all, sem,
):
    j = pl.program_id(0)
    slab = pl.num_programs(0)
    bs = out_ref.shape[1]
    rows = out_ref.shape[0] // bs
    group = f_all.shape[0] // fan
    row_idx, col_idx = lax.axis_index("row"), lax.axis_index("col")

    @pl.when(j == 0)
    def _():
        k = lax.rem(row_idx, fan)
        copies = [pltpu.make_async_copy(mine_hbm, f_all.at[pl.ds(k * group, group)], sem.at[0])]
        for step in range(1, fan):
            at = lax.rem(k + step, fan) * group
            copies.append(
                pltpu.make_async_copy(
                    others_hbm.at[step - 1], f_all.at[pl.ds(at, group)], sem.at[step]
                )
            )
        at = 0
        for piece, part in enumerate((left_hbm, low_hbm, high_hbm, right_hbm)):
            copies.append(
                pltpu.make_async_copy(
                    part, ext.at[:, pl.ds(at, part.shape[1])], sem.at[fan + piece]
                )
            )
            at += part.shape[1]
        for copy in copies:
            copy.start()
        for copy in copies:
            copy.wait()

    col = col_idx * slab + j
    first = col_idx * slab - BAND
    lhs = jnp.concatenate(
        [
            ext[:, pl.ds(pl.multiple_of((cols_ref[e, col] - first) * bs, bs), bs)]
            for e in range(STENCIL)
        ],
        axis=1,
    )
    rhs = jnp.concatenate([f_all[j, e] for e in range(STENCIL)], axis=1)
    spread = lax.dot_general(
        lhs, rhs, (((1,), (1,)), ((), ())), preferred_element_type=jnp.float32
    )
    eye = lax.broadcasted_iota(jnp.int32, (bs, bs), 0) == lax.broadcasted_iota(
        jnp.int32, (bs, bs), 1
    )
    for i in range(rows):
        at = slice(i * bs, (i + 1) * bs)
        keep = mask_ref[i, j].astype(jnp.float32)
        on_main = (row_idx * rows + i == col).astype(jnp.float32)
        noise = jnp.where(eye, q_ref[i : i + 1, :] * on_main, 0.0)
        out_ref[at, :] = w_ref[at, :].astype(jnp.float32) * (spread[at] * keep) + noise


def forecast(
    p_cov, f_blocks, stencil_cols, localization_weights, block_mask, disturbance_variances
):
    rows, cols = lax.axis_size("row"), lax.axis_size("col")
    fan = rows // cols
    block_rows, bs = f_blocks.shape[0], f_blocks.shape[2]
    tall, wide = p_cov.shape
    slab = wide // bs
    halo = BAND * bs
    assert tall == halo and wide == 2 * halo
    cols_of = stencil_cols.T

    up, down = up_down(rows)
    before = lax.ppermute(p_cov, "row", up)
    after = lax.ppermute(p_cov, "row", down)
    held = [f_blocks]
    for source, pairs in group_plan(rows, cols):
        held.append(lax.ppermute(held[source], ("row", "col"), pairs))

    smem = pl.BlockSpec(memory_space=pltpu.SMEM)
    hbm = pl.BlockSpec(memory_space=ANY)
    vmem = pl.BlockSpec(memory_space=pltpu.VMEM)
    p_near, f_near = pl.pallas_call(
        fetch_kernel,
        out_shape=(
            jax.ShapeDtypeStruct(p_cov.shape, p_cov.dtype),
            jax.ShapeDtypeStruct(f_blocks.shape, f_blocks.dtype),
        ),
        in_specs=[hbm, hbm],
        out_specs=(vmem, vmem),
        scratch_shapes=[pltpu.SemaphoreType.DMA((2,))],
        compiler_params=pltpu.CompilerParams(vmem_limit_bytes=8 * 2**20),
        name="fetch",
    )(p_cov, f_blocks)
    half = jax.ShapeDtypeStruct((tall, halo), jnp.bfloat16)
    low, high = pl.pallas_call(
        stage1_kernel,
        out_shape=(half, half),
        in_specs=[smem, vmem, hbm, hbm, hbm],
        out_specs=(vmem, vmem),
        scratch_shapes=[
            pltpu.VMEM((tall + 2 * halo, wide), jnp.bfloat16),
            pltpu.SemaphoreType.DMA((3,)),
        ],
        compiler_params=pltpu.CompilerParams(vmem_limit_bytes=16 * 2**20),
        name="stage1",
    )(cols_of, f_near, before, p_near, after)

    up, down = up_down(cols)
    left = lax.ppermute(high, "col", up)
    right = lax.ppermute(low, "col", down)

    mine = pl.pallas_call(
        functools.partial(pick_kernel, holder_table(rows, cols)),
        out_shape=jax.ShapeDtypeStruct(f_blocks.shape, f_blocks.dtype),
        in_specs=[hbm] * len(held),
        out_specs=vmem,
        scratch_shapes=[pltpu.SemaphoreType.DMA],
        compiler_params=pltpu.CompilerParams(vmem_limit_bytes=4 * 2**20),
        name="pick",
    )(*held)
    others = []
    for step in range(1, fan):
        turn = [(r // fan * fan + (r + step) % fan, r) for r in range(rows)]
        others.append(lax.ppermute(mine, "row", turn))
    others = jnp.stack(others)

    return pl.pallas_call(
        functools.partial(stage2_kernel, fan),
        out_shape=jax.ShapeDtypeStruct((tall, wide), jnp.float32),
        grid=(slab,),
        in_specs=[
            smem,
            smem,
            pl.BlockSpec((block_rows, bs), lambda j: (0, 0)),
            pl.BlockSpec((tall, bs), lambda j: (0, j)),
        ]
        + [hbm] * 6,
        out_specs=pl.BlockSpec((tall, bs), lambda j: (0, j)),
        scratch_shapes=[
            pltpu.VMEM((tall, wide + 2 * halo), jnp.bfloat16),
            pltpu.VMEM((slab, STENCIL, bs, bs), jnp.bfloat16),
            pltpu.SemaphoreType.DMA((4 + fan,)),
        ],
        compiler_params=pltpu.CompilerParams(vmem_limit_bytes=16 * 2**20),
        name="stage2",
    )(
        cols_of,
        block_mask,
        disturbance_variances.reshape(block_rows, bs),
        localization_weights,
        left,
        low,
        high,
        right,
        mine,
        others,
    )


def solution(mesh):
    placed = (
        P("row", "col"),
        P("row", None, None, None),
        P(),
        P("row", "col"),
        P("row", "col"),
        P("row"),
    )
    return jax.shard_map(
        forecast, mesh=mesh, in_specs=placed, out_specs=P("row", "col"), check_vma=False
    )
```

```python
import functools

import jax
import jax.numpy as jnp
from jax import lax
from jax.experimental import pallas as pl
from jax.experimental.pallas import tpu as pltpu
from jax.sharding import PartitionSpec as P


STENCIL = 7
BAND = 4
ANY = pl.ANY


def up_down(devices):
    up = [(i, i + 1) for i in range(devices - 1)]
    return up, [(j, i) for i, j in up]


def source_plane(c, a, cols):
    if cols & (cols - 1):
        return a
    return c ^ (((a ^ c) - 1) % cols)


def group_plan(rows, cols):
    fan = rows // cols

    def at(a, k, c):
        return (a * fan + k) * cols + c

    if (cols, fan) != (4, 2):
        pairs = []
        for c in range(cols):
            for a in range(cols):
                if a != c:
                    plane = source_plane(c, a, cols)
                    pairs += [(at(c, k, plane), at(a, k, c)) for k in range(fan)]
        return [(0, pairs)]
    first, relayed, second = [], [], []
    for c in range(cols):
        near, side, far = c ^ 1, c ^ 2, c ^ 3
        first += [(at(c, 0, c), at(near, 0, c)), (at(c, 1, c), at(side, 1, c))]
        relayed += [(at(near, 0, c), at(far, 0, c)), (at(side, 1, c), at(far, 1, c))]
        second += [(at(c, 0, c), at(side, 0, c)), (at(c, 1, c), at(near, 1, c))]
    return [(0, first), (1, relayed), (0, second)]


def holder_table(rows, cols):
    table = [0] * (rows * cols)
    for step, (_, pairs) in enumerate(group_plan(rows, cols)):
        for _, target in pairs:
            table[target] = step + 1
    return table


def pick_kernel(table, *refs):
    *sources, out_ref, sem = refs
    me = lax.axis_index("row") * lax.axis_size("col") + lax.axis_index("col")
    which = 0
    for device, step in enumerate(table):
        if step:
            which = jnp.where(me == device, step, which)
    for step, source in enumerate(sources):

        @pl.when(which == step)
        def _():
            copy = pltpu.make_async_copy(source, out_ref, sem)
            copy.start()
            copy.wait()


def fetch_kernel(p_hbm, f_hbm, p_ref, f_ref, sem):
    copies = [
        pltpu.make_async_copy(p_hbm, p_ref, sem.at[0]),
        pltpu.make_async_copy(f_hbm, f_ref, sem.at[1]),
    ]
    for copy in copies:
        copy.start()
    for copy in copies:
        copy.wait()


def stage1_kernel(
    cols_ref, f_ref, before_hbm, own_hbm, after_hbm, low_ref, high_ref, ext, sem
):
    rows, bs = f_ref.shape[0], f_ref.shape[2]
    half = low_ref.shape[1]
    first = lax.axis_index("row") * rows
    halo, tall = before_hbm.shape[0], own_hbm.shape[0]
    copies = [
        pltpu.make_async_copy(before_hbm, ext.at[pl.ds(0, halo)], sem.at[0]),
        pltpu.make_async_copy(own_hbm, ext.at[pl.ds(halo, tall)], sem.at[1]),
        pltpu.make_async_copy(after_hbm, ext.at[pl.ds(halo + tall, halo)], sem.at[2]),
    ]
    for copy in copies:
        copy.start()
    for copy in copies:
        copy.wait()
    tile = min(256, half)
    for i in range(rows):
        lhs = jnp.concatenate([f_ref[i, e] for e in range(STENCIL)], axis=1)
        starts = [
            pl.multiple_of((cols_ref[e, first + i] - first + BAND) * bs, bs)
            for e in range(STENCIL)
        ]
        for part, out_ref in enumerate((low_ref, high_ref)):
            for t in range(half // tile):
                at = part * half + t * tile
                rhs = jnp.concatenate(
                    [ext[pl.ds(s, bs), at : at + tile] for s in starts], axis=0
                )
                out_ref[i * bs : (i + 1) * bs, t * tile : (t + 1) * tile] = jnp.dot(
                    lhs, rhs, preferred_element_type=jnp.float32
                ).astype(out_ref.dtype)


def stage2_kernel(fan, turn, cols_ref, mask_ref, q_ref, w_ref, f_hbm, *refs):
    if turn == 0:
        *parts, out_hbm, ext, f_ref, made, f_sem, out_sem, sem = refs
    else:
        ext, _, out_hbm, f_ref, made, f_sem, out_sem = refs
        parts = []
    group, bs = f_hbm.shape[0], f_hbm.shape[2]
    rows, slab = mask_ref.shape
    row_idx, col_idx = lax.axis_index("row"), lax.axis_index("col")
    base = lax.rem(row_idx + turn, fan) * group
    first = col_idx * slab - BAND

    fetches = [
        pltpu.make_async_copy(f_hbm.at[n], f_ref.at[n], f_sem.at[n]) for n in range(group)
    ]
    joins = []
    at = 0
    for piece, part in enumerate(parts):
        to = ext.at[:, pl.ds(at, part.shape[1])]
        joins.append(pltpu.make_async_copy(part, to, sem.at[piece]))
        at += part.shape[1]
    for copy in joins + fetches:
        copy.start()
    for copy in joins + fetches:
        copy.wait()

    eye = lax.broadcasted_iota(jnp.int32, (bs, bs), 0) == lax.broadcasted_iota(
        jnp.int32, (bs, bs), 1
    )
    stores = []
    for n in range(group):
        j = base + n
        col = col_idx * slab + j
        to = pl.ds(pl.multiple_of(j * bs, bs), bs)
        lhs = jnp.concatenate(
            [
                ext[:, pl.ds(pl.multiple_of((cols_ref[e, col] - first) * bs, bs), bs)]
                for e in range(STENCIL)
            ],
            axis=1,
        )
        rhs = jnp.concatenate([f_ref[n, e] for e in range(STENCIL)], axis=1)
        spread = lax.dot_general(
            lhs, rhs, (((1,), (1,)), ((), ())), preferred_element_type=jnp.float32
        )
        for i in range(rows):
            at = slice(i * bs, (i + 1) * bs)
            keep = mask_ref[i, j].astype(jnp.float32)
            on_main = (row_idx * rows + i == col).astype(jnp.float32)
            noise = jnp.where(eye, q_ref[i : i + 1, :] * on_main, 0.0)
            made[n, at, :] = w_ref[at, to].astype(jnp.float32) * (spread[at] * keep) + noise
        store = pltpu.make_async_copy(made.at[n], out_hbm.at[:, to], out_sem.at[n])
        store.start()
        stores.append(store)
    for store in stores:
        store.wait()


def forecast(
    p_cov, f_blocks, stencil_cols, localization_weights, block_mask, disturbance_variances
):
    rows, cols = lax.axis_size("row"), lax.axis_size("col")
    fan = rows // cols
    block_rows, bs = f_blocks.shape[0], f_blocks.shape[2]
    tall, wide = p_cov.shape
    slab = wide // bs
    halo = BAND * bs
    assert tall == halo and wide == 2 * halo
    cols_of = stencil_cols.T

    up, down = up_down(rows)
    before = lax.ppermute(p_cov, "row", up)
    after = lax.ppermute(p_cov, "row", down)
    held = [f_blocks]
    for source, pairs in group_plan(rows, cols):
        held.append(lax.ppermute(held[source], ("row", "col"), pairs))

    smem = pl.BlockSpec(memory_space=pltpu.SMEM)
    hbm = pl.BlockSpec(memory_space=ANY)
    vmem = pl.BlockSpec(memory_space=pltpu.VMEM)
    p_near, f_near = pl.pallas_call(
        fetch_kernel,
        out_shape=(
            jax.ShapeDtypeStruct(p_cov.shape, p_cov.dtype),
            jax.ShapeDtypeStruct(f_blocks.shape, f_blocks.dtype),
        ),
        in_specs=[hbm, hbm],
        out_specs=(vmem, vmem),
        scratch_shapes=[pltpu.SemaphoreType.DMA((2,))],
        compiler_params=pltpu.CompilerParams(vmem_limit_bytes=8 * 2**20),
        name="fetch",
    )(p_cov, f_blocks)
    half = jax.ShapeDtypeStruct((tall, halo), jnp.bfloat16)
    low, high = pl.pallas_call(
        stage1_kernel,
        out_shape=(half, half),
        in_specs=[smem, vmem, hbm, hbm, hbm],
        out_specs=(vmem, vmem),
        scratch_shapes=[
            pltpu.VMEM((tall + 2 * halo, wide), jnp.bfloat16),
            pltpu.SemaphoreType.DMA((3,)),
        ],
        compiler_params=pltpu.CompilerParams(vmem_limit_bytes=16 * 2**20),
        name="stage1",
    )(cols_of, f_near, before, p_near, after)

    up, down = up_down(cols)
    left = lax.ppermute(high, "col", up)
    right = lax.ppermute(low, "col", down)

    mine = pl.pallas_call(
        functools.partial(pick_kernel, holder_table(rows, cols)),
        out_shape=jax.ShapeDtypeStruct(f_blocks.shape, f_blocks.dtype),
        in_specs=[hbm] * len(held),
        out_specs=vmem,
        scratch_shapes=[pltpu.SemaphoreType.DMA],
        compiler_params=pltpu.CompilerParams(vmem_limit_bytes=4 * 2**20),
        name="pick",
    )(*held)
    fixed = (
        cols_of,
        block_mask,
        disturbance_variances.reshape(block_rows, bs),
        localization_weights,
    )
    out_type = jax.ShapeDtypeStruct((tall, wide), jnp.float32)
    group = slab // fan
    scratch = [
        pltpu.VMEM((group, STENCIL, bs, bs), jnp.bfloat16),
        pltpu.VMEM((group, tall, bs), jnp.float32),
        pltpu.SemaphoreType.DMA((group,)),
        pltpu.SemaphoreType.DMA((group,)),
    ]
    params = pltpu.CompilerParams(vmem_limit_bytes=20 * 2**20)
    out, ext = pl.pallas_call(
        functools.partial(stage2_kernel, fan, 0),
        out_shape=(out_type, jax.ShapeDtypeStruct((tall, wide + 2 * halo), jnp.bfloat16)),
        in_specs=[smem, smem, vmem, vmem] + [hbm] * 5,
        out_specs=(pl.BlockSpec(memory_space=pltpu.HBM), vmem),
        scratch_shapes=scratch + [pltpu.SemaphoreType.DMA((4,))],
        compiler_params=params,
        name="stage2",
    )(*fixed, mine, left, low, high, right)
    for turn in range(1, fan):
        pairs = [(r // fan * fan + (r + turn) % fan, r) for r in range(rows)]
        other = lax.ppermute(mine, "row", pairs)
        out = pl.pallas_call(
            functools.partial(stage2_kernel, fan, turn),
            out_shape=out_type,
            in_specs=[smem, smem, vmem, vmem, hbm, vmem, pl.BlockSpec(memory_space=pltpu.HBM)],
            out_specs=pl.BlockSpec(memory_space=pltpu.HBM),
            scratch_shapes=scratch,
            input_output_aliases={6: 0},
            compiler_params=params,
            name="stage3",
        )(*fixed, other, ext, out)
    return out


def solution(mesh):
    placed = (
        P("row", "col"),
        P("row", None, None, None),
        P(),
        P("row", "col"),
        P("row", "col"),
        P("row"),
    )
    return jax.shard_map(
        forecast, mesh=mesh, in_specs=placed, out_specs=P("row", "col"), check_vma=False
    )
```

```python
import functools

import jax
import jax.numpy as jnp
from jax import lax
from jax.experimental import pallas as pl
from jax.experimental.pallas import tpu as pltpu
from jax.sharding import PartitionSpec as P


STENCIL = 7
BAND = 4
ANY = pl.ANY


def up_down(devices):
    up = [(i, i + 1) for i in range(devices - 1)]
    return up, [(j, i) for i, j in up]


def source_plane(c, a, cols):
    if cols & (cols - 1):
        return a
    return c ^ (((a ^ c) - 1) % cols)


def group_plan(rows, cols):
    fan = rows // cols

    def at(a, k, c):
        return (a * fan + k) * cols + c

    if (cols, fan) != (4, 2):
        pairs = []
        for c in range(cols):
            for a in range(cols):
                if a != c:
                    plane = source_plane(c, a, cols)
                    pairs += [(at(c, k, plane), at(a, k, c)) for k in range(fan)]
        return [(0, pairs)]
    first, relayed, second = [], [], []
    for c in range(cols):
        near, side, far = c ^ 1, c ^ 2, c ^ 3
        first += [(at(c, 0, c), at(near, 0, c)), (at(c, 1, c), at(side, 1, c))]
        relayed += [(at(near, 0, c), at(far, 0, c)), (at(side, 1, c), at(far, 1, c))]
        second += [(at(c, 0, c), at(side, 0, c)), (at(c, 1, c), at(near, 1, c))]
    return [(0, first), (1, relayed), (0, second)]


def holder_table(rows, cols):
    table = [0] * (rows * cols)
    for step, (_, pairs) in enumerate(group_plan(rows, cols)):
        for _, target in pairs:
            table[target] = step + 1
    return table


def pick_kernel(table, *refs):
    *sources, out_ref, sem = refs
    me = lax.axis_index("row") * lax.axis_size("col") + lax.axis_index("col")
    which = 0
    for device, step in enumerate(table):
        if step:
            which = jnp.where(me == device, step, which)
    for step, source in enumerate(sources):

        @pl.when(which == step)
        def _():
            copy = pltpu.make_async_copy(source, out_ref, sem)
            copy.start()
            copy.wait()


def fetch_kernel(*refs):
    *ends, sem = refs
    count = len(ends) // 2
    copies = [
        pltpu.make_async_copy(ends[n], ends[count + n], sem.at[n]) for n in range(count)
    ]
    for copy in copies:
        copy.start()
    for copy in copies:
        copy.wait()


def stage1_kernel(
    cols_ref, f_ref, before_hbm, own_hbm, after_hbm, low_ref, high_ref, ext, sem
):
    rows, bs = f_ref.shape[0], f_ref.shape[2]
    half = low_ref.shape[1]
    first = lax.axis_index("row") * rows
    halo, tall = before_hbm.shape[0], own_hbm.shape[0]
    copies = [
        pltpu.make_async_copy(before_hbm, ext.at[pl.ds(0, halo)], sem.at[0]),
        pltpu.make_async_copy(own_hbm, ext.at[pl.ds(halo, tall)], sem.at[1]),
        pltpu.make_async_copy(after_hbm, ext.at[pl.ds(halo + tall, halo)], sem.at[2]),
    ]
    for copy in copies:
        copy.start()
    for copy in copies:
        copy.wait()
    tile = min(256, half)
    for i in range(rows):
        lhs = jnp.concatenate([f_ref[i, e] for e in range(STENCIL)], axis=1)
        starts = [
            pl.multiple_of((cols_ref[e, first + i] - first + BAND) * bs, bs)
            for e in range(STENCIL)
        ]
        for part, out_ref in enumerate((low_ref, high_ref)):
            for t in range(half // tile):
                at = part * half + t * tile
                rhs = jnp.concatenate(
                    [ext[pl.ds(s, bs), at : at + tile] for s in starts], axis=0
                )
                out_ref[i * bs : (i + 1) * bs, t * tile : (t + 1) * tile] = jnp.dot(
                    lhs, rhs, preferred_element_type=jnp.float32
                ).astype(out_ref.dtype)


def stage2_kernel(fan, turn, cols_ref, mask_ref, q_ref, w_ref, f_ref, *refs):
    if turn == 0:
        *parts, out_hbm, ext, made, out_sem, sem = refs
    else:
        ext, _, out_hbm, made, out_sem = refs
        parts = []
    group, bs = f_ref.shape[0], f_ref.shape[2]
    rows, slab = mask_ref.shape
    row_idx, col_idx = lax.axis_index("row"), lax.axis_index("col")
    base = lax.rem(row_idx + turn, fan) * group
    first = col_idx * slab - BAND

    joins = []
    at = 0
    for piece, part in enumerate(parts):
        to = ext.at[:, pl.ds(at, part.shape[1])]
        joins.append(pltpu.make_async_copy(part, to, sem.at[piece]))
        at += part.shape[1]
    for copy in joins:
        copy.start()
    for copy in joins:
        copy.wait()

    eye = lax.broadcasted_iota(jnp.int32, (bs, bs), 0) == lax.broadcasted_iota(
        jnp.int32, (bs, bs), 1
    )
    stores = []
    for n in range(group):
        j = base + n
        col = col_idx * slab + j
        to = pl.ds(pl.multiple_of(j * bs, bs), bs)
        lhs = jnp.concatenate(
            [
                ext[:, pl.ds(pl.multiple_of((cols_ref[e, col] - first) * bs, bs), bs)]
                for e in range(STENCIL)
            ],
            axis=1,
        )
        rhs = jnp.concatenate([f_ref[n, e] for e in range(STENCIL)], axis=1)
        spread = lax.dot_general(
            lhs, rhs, (((1,), (1,)), ((), ())), preferred_element_type=jnp.float32
        )
        for i in range(rows):
            at = slice(i * bs, (i + 1) * bs)
            keep = mask_ref[i, j].astype(jnp.float32)
            on_main = (row_idx * rows + i == col).astype(jnp.float32)
            noise = jnp.where(eye, q_ref[i : i + 1, :] * on_main, 0.0)
            made[n, at, :] = w_ref[at, to].astype(jnp.float32) * (spread[at] * keep) + noise
        store = pltpu.make_async_copy(made.at[n], out_hbm.at[:, to], out_sem.at[n])
        store.start()
        stores.append(store)
    for store in stores:
        store.wait()


def forecast(
    p_cov, f_blocks, stencil_cols, localization_weights, block_mask, disturbance_variances
):
    rows, cols = lax.axis_size("row"), lax.axis_size("col")
    fan = rows // cols
    block_rows, bs = f_blocks.shape[0], f_blocks.shape[2]
    tall, wide = p_cov.shape
    slab = wide // bs
    halo = BAND * bs
    assert tall == halo and wide == 2 * halo
    cols_of = stencil_cols.T

    up, down = up_down(rows)
    before = lax.ppermute(p_cov, "row", up)
    after = lax.ppermute(p_cov, "row", down)
    held = [f_blocks]
    for source, pairs in group_plan(rows, cols):
        held.append(lax.ppermute(held[source], ("row", "col"), pairs))

    smem = pl.BlockSpec(memory_space=pltpu.SMEM)
    hbm = pl.BlockSpec(memory_space=ANY)
    vmem = pl.BlockSpec(memory_space=pltpu.VMEM)
    wanted = (p_cov, f_blocks, cols_of)
    p_near, f_near, cols_of = pl.pallas_call(
        fetch_kernel,
        out_shape=tuple(jax.ShapeDtypeStruct(x.shape, x.dtype) for x in wanted),
        in_specs=[hbm] * len(wanted),
        out_specs=(vmem,) * len(wanted),
        scratch_shapes=[pltpu.SemaphoreType.DMA((len(wanted),))],
        compiler_params=pltpu.CompilerParams(vmem_limit_bytes=8 * 2**20),
        name="fetch",
    )(*wanted)
    half = jax.ShapeDtypeStruct((tall, halo), jnp.bfloat16)
    low, high = pl.pallas_call(
        stage1_kernel,
        out_shape=(half, half),
        in_specs=[smem, vmem, hbm, hbm, hbm],
        out_specs=(vmem, vmem),
        scratch_shapes=[
            pltpu.VMEM((tall + 2 * halo, wide), jnp.bfloat16),
            pltpu.SemaphoreType.DMA((3,)),
        ],
        compiler_params=pltpu.CompilerParams(vmem_limit_bytes=16 * 2**20),
        name="stage1",
    )(cols_of, f_near, before, p_near, after)

    up, down = up_down(cols)
    left = lax.ppermute(high, "col", up)
    right = lax.ppermute(low, "col", down)

    mine = pl.pallas_call(
        functools.partial(pick_kernel, holder_table(rows, cols)),
        out_shape=jax.ShapeDtypeStruct(f_blocks.shape, f_blocks.dtype),
        in_specs=[hbm] * len(held),
        out_specs=vmem,
        scratch_shapes=[pltpu.SemaphoreType.DMA],
        compiler_params=pltpu.CompilerParams(vmem_limit_bytes=4 * 2**20),
        name="pick",
    )(*held)
    fixed = (
        cols_of,
        block_mask,
        disturbance_variances.reshape(block_rows, bs),
        localization_weights,
    )
    out_type = jax.ShapeDtypeStruct((tall, wide), jnp.float32)
    group = slab // fan
    scratch = [
        pltpu.VMEM((group, tall, bs), jnp.float32),
        pltpu.SemaphoreType.DMA((group,)),
    ]
    params = pltpu.CompilerParams(vmem_limit_bytes=20 * 2**20)
    out, ext = pl.pallas_call(
        functools.partial(stage2_kernel, fan, 0),
        out_shape=(out_type, jax.ShapeDtypeStruct((tall, wide + 2 * halo), jnp.bfloat16)),
        in_specs=[smem, smem, vmem, vmem, vmem] + [hbm] * 4,
        out_specs=(pl.BlockSpec(memory_space=pltpu.HBM), vmem),
        scratch_shapes=scratch + [pltpu.SemaphoreType.DMA((4,))],
        compiler_params=params,
        name="stage2",
    )(*fixed, mine, left, low, high, right)
    for turn in range(1, fan):
        pairs = [(r // fan * fan + (r + turn) % fan, r) for r in range(rows)]
        other = lax.ppermute(mine, "row", pairs)
        out = pl.pallas_call(
            functools.partial(stage2_kernel, fan, turn),
            out_shape=out_type,
            in_specs=[smem, smem, vmem, vmem, vmem, vmem, pl.BlockSpec(memory_space=pltpu.HBM)],
            out_specs=pl.BlockSpec(memory_space=pltpu.HBM),
            scratch_shapes=scratch,
            input_output_aliases={6: 0},
            compiler_params=params,
            name="stage3",
        )(*fixed, other, ext, out)
    return out


def solution(mesh):
    placed = (
        P("row", "col"),
        P("row", None, None, None),
        P(),
        P("row", "col"),
        P("row", "col"),
        P("row"),
    )
    return jax.shard_map(
        forecast, mesh=mesh, in_specs=placed, out_specs=P("row", "col"), check_vma=False
    )
```

```python
import functools

import jax
import jax.numpy as jnp
from jax import lax
from jax.experimental import pallas as pl
from jax.experimental.pallas import tpu as pltpu
from jax.sharding import PartitionSpec as P


STENCIL = 7
BAND = 4
ANY = pl.ANY


def up_down(devices):
    up = [(i, i + 1) for i in range(devices - 1)]
    return up, [(j, i) for i, j in up]


def source_plane(c, a, cols):
    if cols & (cols - 1):
        return a
    return c ^ (((a ^ c) - 1) % cols)


def group_plan(rows, cols):
    fan = rows // cols

    def at(a, k, c):
        return (a * fan + k) * cols + c

    if (cols, fan) != (4, 2):
        pairs = []
        for c in range(cols):
            for a in range(cols):
                if a != c:
                    plane = source_plane(c, a, cols)
                    pairs += [(at(c, k, plane), at(a, k, c)) for k in range(fan)]
        return [(0, pairs)]
    first, relayed, second = [], [], []
    for c in range(cols):
        near, side, far = c ^ 1, c ^ 2, c ^ 3
        first += [(at(c, 0, c), at(near, 0, c)), (at(c, 1, c), at(side, 1, c))]
        relayed += [(at(near, 0, c), at(far, 0, c)), (at(side, 1, c), at(far, 1, c))]
        second += [(at(c, 0, c), at(side, 0, c)), (at(c, 1, c), at(near, 1, c))]
    return [(0, first), (1, relayed), (0, second)]


def holder_table(rows, cols):
    table = [0] * (rows * cols)
    for step, (_, pairs) in enumerate(group_plan(rows, cols)):
        for _, target in pairs:
            table[target] = step + 1
    return table


def pick_kernel(table, *refs):
    *sources, out_ref, sem = refs
    me = lax.axis_index("row") * lax.axis_size("col") + lax.axis_index("col")
    which = 0
    for device, step in enumerate(table):
        if step:
            which = jnp.where(me == device, step, which)
    for step, source in enumerate(sources):

        @pl.when(which == step)
        def _():
            copy = pltpu.make_async_copy(source, out_ref, sem)
            copy.start()
            copy.wait()


def fetch_kernel(p_hbm, f_hbm, cols_hbm, top_ref, bottom_ref, f_ref, cols_ref, sem):
    half = top_ref.shape[0]
    copies = [
        pltpu.make_async_copy(p_hbm.at[:half], top_ref, sem.at[0]),
        pltpu.make_async_copy(p_hbm.at[half:], bottom_ref, sem.at[1]),
        pltpu.make_async_copy(f_hbm, f_ref, sem.at[2]),
        pltpu.make_async_copy(cols_hbm, cols_ref, sem.at[3]),
    ]
    for copy in copies:
        copy.start()
    for copy in copies:
        copy.wait()


def stage1_kernel(bent, cols_ref, f_ref, top_hbm, bottom_hbm, before_hbm, after_hbm, *refs):
    *halves, low_ref, high_ref, ext, sem = refs
    rows, bs = f_ref.shape[0], f_ref.shape[2]
    half = low_ref.shape[1]
    row_idx = lax.axis_index("row")
    first = row_idx * rows
    halo, part = before_hbm.shape[0], top_hbm.shape[0]

    def copies(at, pieces, sems):
        for piece, n in zip(pieces, sems):
            yield pltpu.make_async_copy(piece, ext.at[pl.ds(at, piece.shape[0])], sem.at[n])
            at += piece.shape[0]

    def all_copies(act):
        for copy in copies(halo, (top_hbm, bottom_hbm), (0, 1)):
            act(copy)
        for at, whole, device, n in ((0, before_hbm, 0, 2), (halo + 2 * part, after_hbm, 1, 4)):
            if not halves:
                for copy in copies(at, (whole,), (n,)):
                    act(copy)
                continue

            @pl.when(row_idx != bent[device])
            def _():
                for copy in copies(at, (whole,), (n,)):
                    act(copy)

            @pl.when(row_idx == bent[device])
            def _():
                for copy in copies(at, halves, (n, n + 1)):
                    act(copy)

    all_copies(lambda copy: copy.start())
    all_copies(lambda copy: copy.wait())
    tile = min(256, half)
    for i in range(rows):
        lhs = jnp.concatenate([f_ref[i, e] for e in range(STENCIL)], axis=1)
        starts = [
            pl.multiple_of((cols_ref[e, first + i] - first + BAND) * bs, bs)
            for e in range(STENCIL)
        ]
        for part, out_ref in enumerate((low_ref, high_ref)):
            for t in range(half // tile):
                at = part * half + t * tile
                rhs = jnp.concatenate(
                    [ext[pl.ds(s, bs), at : at + tile] for s in starts], axis=0
                )
                out_ref[i * bs : (i + 1) * bs, t * tile : (t + 1) * tile] = jnp.dot(
                    lhs, rhs, preferred_element_type=jnp.float32
                ).astype(out_ref.dtype)


def stage2_kernel(fan, turn, cols_ref, mask_ref, q_ref, w_ref, f_ref, *refs):
    if turn == 0:
        *parts, out_hbm, ext, made, out_sem, sem = refs
    else:
        ext, _, out_hbm, made, out_sem = refs
        parts = []
    group, bs = f_ref.shape[0], f_ref.shape[2]
    rows, slab = mask_ref.shape
    row_idx, col_idx = lax.axis_index("row"), lax.axis_index("col")
    base = lax.rem(row_idx + turn, fan) * group
    first = col_idx * slab - BAND

    joins = []
    at = 0
    for piece, part in enumerate(parts):
        to = ext.at[:, pl.ds(at, part.shape[1])]
        joins.append(pltpu.make_async_copy(part, to, sem.at[piece]))
        at += part.shape[1]
    for copy in joins:
        copy.start()
    for copy in joins:
        copy.wait()

    eye = lax.broadcasted_iota(jnp.int32, (bs, bs), 0) == lax.broadcasted_iota(
        jnp.int32, (bs, bs), 1
    )
    stores = []
    for n in range(group):
        j = base + n
        col = col_idx * slab + j
        to = pl.ds(pl.multiple_of(j * bs, bs), bs)
        lhs = jnp.concatenate(
            [
                ext[:, pl.ds(pl.multiple_of((cols_ref[e, col] - first) * bs, bs), bs)]
                for e in range(STENCIL)
            ],
            axis=1,
        )
        rhs = jnp.concatenate([f_ref[n, e] for e in range(STENCIL)], axis=1)
        spread = lax.dot_general(
            lhs, rhs, (((1,), (1,)), ((), ())), preferred_element_type=jnp.float32
        )
        for i in range(rows):
            at = slice(i * bs, (i + 1) * bs)
            keep = mask_ref[i, j].astype(jnp.float32)
            on_main = (row_idx * rows + i == col).astype(jnp.float32)
            noise = jnp.where(eye, q_ref[i : i + 1, :] * on_main, 0.0)
            made[n, at, :] = w_ref[at, to].astype(jnp.float32) * (spread[at] * keep) + noise
        store = pltpu.make_async_copy(made.at[n], out_hbm.at[:, to], out_sem.at[n])
        store.start()
        stores.append(store)
    for store in stores:
        store.wait()


def forecast(
    p_cov, f_blocks, stencil_cols, localization_weights, block_mask, disturbance_variances
):
    rows, cols = lax.axis_size("row"), lax.axis_size("col")
    fan = rows // cols
    block_rows, bs = f_blocks.shape[0], f_blocks.shape[2]
    tall, wide = p_cov.shape
    slab = wide // bs
    halo = BAND * bs
    assert tall == halo and wide == 2 * halo
    cols_of = stencil_cols.T

    smem = pl.BlockSpec(memory_space=pltpu.SMEM)
    hbm = pl.BlockSpec(memory_space=ANY)
    vmem = pl.BlockSpec(memory_space=pltpu.VMEM)
    wanted = (
        jax.ShapeDtypeStruct((tall // 2, wide), p_cov.dtype),
        jax.ShapeDtypeStruct((tall // 2, wide), p_cov.dtype),
        jax.ShapeDtypeStruct(f_blocks.shape, f_blocks.dtype),
        jax.ShapeDtypeStruct(cols_of.shape, cols_of.dtype),
    )
    top, bottom, f_near, cols_of = pl.pallas_call(
        fetch_kernel,
        out_shape=wanted,
        in_specs=[hbm] * 3,
        out_specs=(vmem,) * 4,
        scratch_shapes=[pltpu.SemaphoreType.DMA((4,))],
        compiler_params=pltpu.CompilerParams(vmem_limit_bytes=8 * 2**20),
        name="fetch",
    )(p_cov, f_blocks, cols_of)

    up, down = up_down(rows)
    bent, halves = (rows // 2, rows // 2 - 1), ()
    if (cols, fan) == (4, 2):
        lower, upper = bent
        across = [(upper, lower), (lower, upper)]
        up, down = (
            [pair for pair in pairs if pair not in across] for pairs in (up, down)
        )
        straight = lax.ppermute(top, "row", across)
        turn = lax.ppermute(bottom, "row", [(upper, rows - 1), (lower, 0)])
        turned = lax.ppermute(turn, "row", [(rows - 1, lower), (0, upper)])
        halves = (straight, turned)
    before = lax.ppermute(p_cov, "row", up)
    after = lax.ppermute(p_cov, "row", down)
    held = [f_blocks]
    for source, pairs in group_plan(rows, cols):
        held.append(lax.ppermute(held[source], ("row", "col"), pairs))

    half = jax.ShapeDtypeStruct((tall, halo), jnp.bfloat16)
    low, high = pl.pallas_call(
        functools.partial(stage1_kernel, bent),
        out_shape=(half, half),
        in_specs=[smem, vmem] + [hbm] * (4 + len(halves)),
        out_specs=(vmem, vmem),
        scratch_shapes=[
            pltpu.VMEM((tall + 2 * halo, wide), jnp.bfloat16),
            pltpu.SemaphoreType.DMA((6,)),
        ],
        compiler_params=pltpu.CompilerParams(vmem_limit_bytes=16 * 2**20),
        name="stage1",
    )(cols_of, f_near, top, bottom, before, after, *halves)

    up, down = up_down(cols)
    left = lax.ppermute(high, "col", up)
    right = lax.ppermute(low, "col", down)

    mine = pl.pallas_call(
        functools.partial(pick_kernel, holder_table(rows, cols)),
        out_shape=jax.ShapeDtypeStruct(f_blocks.shape, f_blocks.dtype),
        in_specs=[hbm] * len(held),
        out_specs=vmem,
        scratch_shapes=[pltpu.SemaphoreType.DMA],
        compiler_params=pltpu.CompilerParams(vmem_limit_bytes=4 * 2**20),
        name="pick",
    )(*held)
    fixed = (
        cols_of,
        block_mask,
        disturbance_variances.reshape(block_rows, bs),
        localization_weights,
    )
    out_type = jax.ShapeDtypeStruct((tall, wide), jnp.float32)
    group = slab // fan
    scratch = [
        pltpu.VMEM((group, tall, bs), jnp.float32),
        pltpu.SemaphoreType.DMA((group,)),
    ]
    params = pltpu.CompilerParams(vmem_limit_bytes=20 * 2**20)
    out, ext = pl.pallas_call(
        functools.partial(stage2_kernel, fan, 0),
        out_shape=(out_type, jax.ShapeDtypeStruct((tall, wide + 2 * halo), jnp.bfloat16)),
        in_specs=[smem, smem, vmem, vmem, vmem] + [hbm] * 4,
        out_specs=(pl.BlockSpec(memory_space=pltpu.HBM), vmem),
        scratch_shapes=scratch + [pltpu.SemaphoreType.DMA((4,))],
        compiler_params=params,
        name="stage2",
    )(*fixed, mine, left, low, high, right)
    for turn in range(1, fan):
        pairs = [(r // fan * fan + (r + turn) % fan, r) for r in range(rows)]
        other = lax.ppermute(mine, "row", pairs)
        out = pl.pallas_call(
            functools.partial(stage2_kernel, fan, turn),
            out_shape=out_type,
            in_specs=[smem, smem, vmem, vmem, vmem, vmem, pl.BlockSpec(memory_space=pltpu.HBM)],
            out_specs=pl.BlockSpec(memory_space=pltpu.HBM),
            scratch_shapes=scratch,
            input_output_aliases={6: 0},
            compiler_params=params,
            name="stage3",
        )(*fixed, other, ext, out)
    return out


def solution(mesh):
    placed = (
        P("row", "col"),
        P("row", None, None, None),
        P(),
        P("row", "col"),
        P("row", "col"),
        P("row"),
    )
    return jax.shard_map(
        forecast, mesh=mesh, in_specs=placed, out_specs=P("row", "col"), check_vma=False
    )
```

```python
import functools

import jax
import jax.numpy as jnp
from jax import lax
from jax.experimental import pallas as pl
from jax.experimental.pallas import tpu as pltpu
from jax.sharding import PartitionSpec as P


STENCIL = 7
BAND = 4
ANY = pl.ANY


def up_down(devices):
    up = [(i, i + 1) for i in range(devices - 1)]
    return up, [(j, i) for i, j in up]


def source_plane(c, a, cols):
    if cols & (cols - 1):
        return a
    return c ^ (((a ^ c) - 1) % cols)


def group_plan(rows, cols):
    fan = rows // cols

    def at(a, k, c):
        return (a * fan + k) * cols + c

    if (cols, fan) != (4, 2):
        pairs = []
        for c in range(cols):
            for a in range(cols):
                if a != c:
                    plane = source_plane(c, a, cols)
                    pairs += [(at(c, k, plane), at(a, k, c)) for k in range(fan)]
        return [(0, pairs)]
    first, relayed, second = [], [], []
    for c in range(cols):
        near, side, far = c ^ 1, c ^ 2, c ^ 3
        first += [(at(c, 0, c), at(near, 0, c)), (at(c, 1, c), at(side, 1, c))]
        relayed += [(at(near, 0, c), at(far, 0, c)), (at(side, 1, c), at(far, 1, c))]
        second += [(at(c, 0, c), at(side, 0, c)), (at(c, 1, c), at(near, 1, c))]
    return [(0, first), (1, relayed), (0, second)]


def holder_table(rows, cols):
    table = [0] * (rows * cols)
    for step, (_, pairs) in enumerate(group_plan(rows, cols)):
        for _, target in pairs:
            table[target] = step + 1
    return table


def pick_kernel(table, *refs):
    *sources, out_ref, sem = refs
    me = lax.axis_index("row") * lax.axis_size("col") + lax.axis_index("col")
    which = 0
    for device, step in enumerate(table):
        if step:
            which = jnp.where(me == device, step, which)
    for step, source in enumerate(sources):

        @pl.when(which == step)
        def _():
            copy = pltpu.make_async_copy(source, out_ref, sem)
            copy.start()
            copy.wait()


def fetch_kernel(f_hbm, cols_hbm, f_ref, cols_ref, sem):
    copies = [
        pltpu.make_async_copy(f_hbm, f_ref, sem.at[0]),
        pltpu.make_async_copy(cols_hbm, cols_ref, sem.at[1]),
    ]
    for copy in copies:
        copy.start()
    for copy in copies:
        copy.wait()


def stage1_kernel(bent, cols_ref, f_ref, top_hbm, bottom_hbm, before_hbm, after_hbm, *refs):
    *halves, low_ref, high_ref, ext, sem = refs
    rows, bs = f_ref.shape[0], f_ref.shape[2]
    half = low_ref.shape[1]
    row_idx = lax.axis_index("row")
    first = row_idx * rows
    halo, part = before_hbm.shape[0], top_hbm.shape[0]

    def copies(at, pieces, sems):
        for piece, n in zip(pieces, sems):
            yield pltpu.make_async_copy(piece, ext.at[pl.ds(at, piece.shape[0])], sem.at[n])
            at += piece.shape[0]

    def all_copies(act):
        for copy in copies(halo, (top_hbm, bottom_hbm), (0, 1)):
            act(copy)
        for at, whole, device, n in ((0, before_hbm, 0, 2), (halo + 2 * part, after_hbm, 1, 4)):
            if not halves:
                for copy in copies(at, (whole,), (n,)):
                    act(copy)
                continue

            @pl.when(row_idx != bent[device])
            def _():
                for copy in copies(at, (whole,), (n,)):
                    act(copy)

            @pl.when(row_idx == bent[device])
            def _():
                for copy in copies(at, halves, (n, n + 1)):
                    act(copy)

    all_copies(lambda copy: copy.start())
    all_copies(lambda copy: copy.wait())
    tile = min(256, half)
    for i in range(rows):
        lhs = jnp.concatenate([f_ref[i, e] for e in range(STENCIL)], axis=1)
        starts = [
            pl.multiple_of((cols_ref[e, first + i] - first + BAND) * bs, bs)
            for e in range(STENCIL)
        ]
        for part, out_ref in enumerate((low_ref, high_ref)):
            for t in range(half // tile):
                at = part * half + t * tile
                rhs = jnp.concatenate(
                    [ext[pl.ds(s, bs), at : at + tile] for s in starts], axis=0
                )
                out_ref[i * bs : (i + 1) * bs, t * tile : (t + 1) * tile] = jnp.dot(
                    lhs, rhs, preferred_element_type=jnp.float32
                ).astype(out_ref.dtype)


def stage2_kernel(fan, turn, cols_ref, mask_ref, q_ref, w_ref, f_ref, *refs):
    if turn == 0:
        *parts, out_hbm, ext, made, out_sem, sem = refs
    else:
        ext, _, out_hbm, made, out_sem = refs
        parts = []
    group, bs = f_ref.shape[0], f_ref.shape[2]
    rows, slab = mask_ref.shape
    row_idx, col_idx = lax.axis_index("row"), lax.axis_index("col")
    base = lax.rem(row_idx + turn, fan) * group
    first = col_idx * slab - BAND

    joins = []
    at = 0
    for piece, part in enumerate(parts):
        to = ext.at[:, pl.ds(at, part.shape[1])]
        joins.append(pltpu.make_async_copy(part, to, sem.at[piece]))
        at += part.shape[1]
    for copy in joins:
        copy.start()
    for copy in joins:
        copy.wait()

    eye = lax.broadcasted_iota(jnp.int32, (bs, bs), 0) == lax.broadcasted_iota(
        jnp.int32, (bs, bs), 1
    )
    stores = []
    for n in range(group):
        j = base + n
        col = col_idx * slab + j
        to = pl.ds(pl.multiple_of(j * bs, bs), bs)
        lhs = jnp.concatenate(
            [
                ext[:, pl.ds(pl.multiple_of((cols_ref[e, col] - first) * bs, bs), bs)]
                for e in range(STENCIL)
            ],
            axis=1,
        )
        rhs = jnp.concatenate([f_ref[n, e] for e in range(STENCIL)], axis=1)
        spread = lax.dot_general(
            lhs, rhs, (((1,), (1,)), ((), ())), preferred_element_type=jnp.float32
        )
        for i in range(rows):
            at = slice(i * bs, (i + 1) * bs)
            keep = mask_ref[i, j].astype(jnp.float32)
            on_main = (row_idx * rows + i == col).astype(jnp.float32)
            noise = jnp.where(eye, q_ref[i : i + 1, :] * on_main, 0.0)
            made[n, at, :] = w_ref[at, to].astype(jnp.float32) * (spread[at] * keep) + noise
        store = pltpu.make_async_copy(made.at[n], out_hbm.at[:, to], out_sem.at[n])
        store.start()
        stores.append(store)
    for store in stores:
        store.wait()


def forecast(
    p_cov, f_blocks, stencil_cols, localization_weights, block_mask, disturbance_variances
):
    rows, cols = lax.axis_size("row"), lax.axis_size("col")
    fan = rows // cols
    block_rows, bs = f_blocks.shape[0], f_blocks.shape[2]
    tall, wide = p_cov.shape
    slab = wide // bs
    halo = BAND * bs
    assert tall == halo and wide == 2 * halo
    cols_of = stencil_cols.T

    smem = pl.BlockSpec(memory_space=pltpu.SMEM)
    hbm = pl.BlockSpec(memory_space=ANY)
    vmem = pl.BlockSpec(memory_space=pltpu.VMEM)
    top, bottom = p_cov[: tall // 2], p_cov[tall // 2 :]
    f_near, cols_of = pl.pallas_call(
        fetch_kernel,
        out_shape=tuple(jax.ShapeDtypeStruct(x.shape, x.dtype) for x in (f_blocks, cols_of)),
        in_specs=[hbm, hbm],
        out_specs=(vmem, vmem),
        scratch_shapes=[pltpu.SemaphoreType.DMA((2,))],
        compiler_params=pltpu.CompilerParams(vmem_limit_bytes=8 * 2**20),
        name="fetch",
    )(f_blocks, cols_of)

    up, down = up_down(rows)
    bent, halves = (rows // 2, rows // 2 - 1), ()
    if (cols, fan) == (4, 2):
        lower, upper = bent
        across = [(upper, lower), (lower, upper)]
        up, down = (
            [pair for pair in pairs if pair not in across] for pairs in (up, down)
        )
        straight = lax.ppermute(top, "row", across)
        turn = lax.ppermute(bottom, "row", [(upper, rows - 1), (lower, 0)])
        turned = lax.ppermute(turn, "row", [(rows - 1, lower), (0, upper)])
        halves = (straight, turned)
    before = lax.ppermute(p_cov, "row", up)
    after = lax.ppermute(p_cov, "row", down)
    held = [f_blocks]
    for source, pairs in group_plan(rows, cols):
        held.append(lax.ppermute(held[source], ("row", "col"), pairs))

    half = jax.ShapeDtypeStruct((tall, halo), jnp.bfloat16)
    low, high = pl.pallas_call(
        functools.partial(stage1_kernel, bent),
        out_shape=(half, half),
        in_specs=[smem, vmem] + [hbm] * (4 + len(halves)),
        out_specs=(vmem, vmem),
        scratch_shapes=[
            pltpu.VMEM((tall + 2 * halo, wide), jnp.bfloat16),
            pltpu.SemaphoreType.DMA((6,)),
        ],
        compiler_params=pltpu.CompilerParams(vmem_limit_bytes=16 * 2**20),
        name="stage1",
    )(cols_of, f_near, top, bottom, before, after, *halves)

    up, down = up_down(cols)
    left = lax.ppermute(high, "col", up)
    right = lax.ppermute(low, "col", down)

    mine = pl.pallas_call(
        functools.partial(pick_kernel, holder_table(rows, cols)),
        out_shape=jax.ShapeDtypeStruct(f_blocks.shape, f_blocks.dtype),
        in_specs=[hbm] * len(held),
        out_specs=vmem,
        scratch_shapes=[pltpu.SemaphoreType.DMA],
        compiler_params=pltpu.CompilerParams(vmem_limit_bytes=4 * 2**20),
        name="pick",
    )(*held)
    fixed = (
        cols_of,
        block_mask,
        disturbance_variances.reshape(block_rows, bs),
        localization_weights,
    )
    out_type = jax.ShapeDtypeStruct((tall, wide), jnp.float32)
    group = slab // fan
    scratch = [
        pltpu.VMEM((group, tall, bs), jnp.float32),
        pltpu.SemaphoreType.DMA((group,)),
    ]
    params = pltpu.CompilerParams(vmem_limit_bytes=20 * 2**20)
    out, ext = pl.pallas_call(
        functools.partial(stage2_kernel, fan, 0),
        out_shape=(out_type, jax.ShapeDtypeStruct((tall, wide + 2 * halo), jnp.bfloat16)),
        in_specs=[smem, smem, vmem, vmem, vmem] + [hbm] * 4,
        out_specs=(pl.BlockSpec(memory_space=pltpu.HBM), vmem),
        scratch_shapes=scratch + [pltpu.SemaphoreType.DMA((4,))],
        compiler_params=params,
        name="stage2",
    )(*fixed, mine, left, low, high, right)
    for turn in range(1, fan):
        pairs = [(r // fan * fan + (r + turn) % fan, r) for r in range(rows)]
        other = lax.ppermute(mine, "row", pairs)
        out = pl.pallas_call(
            functools.partial(stage2_kernel, fan, turn),
            out_shape=out_type,
            in_specs=[smem, smem, vmem, vmem, vmem, vmem, pl.BlockSpec(memory_space=pltpu.HBM)],
            out_specs=pl.BlockSpec(memory_space=pltpu.HBM),
            scratch_shapes=scratch,
            input_output_aliases={6: 0},
            compiler_params=params,
            name="stage3",
        )(*fixed, other, ext, out)
    return out


def solution(mesh):
    placed = (
        P("row", "col"),
        P("row", None, None, None),
        P(),
        P("row", "col"),
        P("row", "col"),
        P("row"),
    )
    return jax.shard_map(
        forecast, mesh=mesh, in_specs=placed, out_specs=P("row", "col"), check_vma=False
    )
```

```python
import functools

import jax
import jax.numpy as jnp
from jax import lax
from jax.experimental import pallas as pl
from jax.experimental.pallas import tpu as pltpu
from jax.sharding import PartitionSpec as P


STENCIL = 7
BAND = 4
ANY = pl.ANY


def exchanges(devices):
    both = []
    for start in (0, 1):
        pairs = [(i, i + 1) for i in range(start, devices - 1, 2)]
        both.append(pairs + [(j, i) for i, j in pairs])
    return both


def source_plane(c, a, cols):
    if cols & (cols - 1):
        return a
    return c ^ (((a ^ c) - 1) % cols)


def group_plan(rows, cols):
    fan = rows // cols

    def at(a, k, c):
        return (a * fan + k) * cols + c

    if (cols, fan) != (4, 2):
        pairs = []
        for c in range(cols):
            for a in range(cols):
                if a != c:
                    plane = source_plane(c, a, cols)
                    pairs += [(at(c, k, plane), at(a, k, c)) for k in range(fan)]
        return [(0, pairs)]
    first, relayed, second = [], [], []
    for c in range(cols):
        near, side, far = c ^ 1, c ^ 2, c ^ 3
        first += [(at(c, 0, c), at(near, 0, c)), (at(c, 1, c), at(side, 1, c))]
        relayed += [(at(near, 0, c), at(far, 0, c)), (at(side, 1, c), at(far, 1, c))]
        second += [(at(c, 0, c), at(side, 0, c)), (at(c, 1, c), at(near, 1, c))]
    return [(0, first), (1, relayed), (0, second)]


def holder_table(rows, cols):
    table = [0] * (rows * cols)
    for step, (_, pairs) in enumerate(group_plan(rows, cols)):
        for _, target in pairs:
            table[target] = step + 1
    return table


def pick_kernel(table, *refs):
    *sources, out_ref, sem = refs
    me = lax.axis_index("row") * lax.axis_size("col") + lax.axis_index("col")
    which = 0
    for device, step in enumerate(table):
        if step:
            which = jnp.where(me == device, step, which)
    for step, source in enumerate(sources):

        @pl.when(which == step)
        def _():
            copy = pltpu.make_async_copy(source, out_ref, sem)
            copy.start()
            copy.wait()


def fetch_kernel(f_hbm, cols_hbm, f_ref, cols_ref, sem):
    copies = [
        pltpu.make_async_copy(f_hbm, f_ref, sem.at[0]),
        pltpu.make_async_copy(cols_hbm, cols_ref, sem.at[1]),
    ]
    for copy in copies:
        copy.start()
    for copy in copies:
        copy.wait()


def stage1_kernel(bent, cols_ref, f_ref, top_hbm, bottom_hbm, inner_hbm, outer_hbm, *refs):
    *halves, first_ref, second_ref, ext, sem = refs
    rows, bs = f_ref.shape[0], f_ref.shape[2]
    half = first_ref.shape[1]
    row_idx, col_idx = lax.axis_index("row"), lax.axis_index("col")
    base = row_idx * rows
    halo, part = inner_hbm.shape[0], top_hbm.shape[0]
    below = halo + 2 * part
    odd = lax.rem(row_idx, 2)
    inner_at = pl.multiple_of((1 - odd) * below, bs)
    outer_at = pl.multiple_of(odd * below, bs)

    def copies(at, pieces, sems):
        for piece, n in zip(pieces, sems):
            yield pltpu.make_async_copy(piece, ext.at[pl.ds(at, piece.shape[0])], sem.at[n])
            at += piece.shape[0]

    def all_copies(act):
        for copy in copies(halo, (top_hbm, bottom_hbm), (0, 1)):
            act(copy)
        for copy in copies(inner_at, (inner_hbm,), (2,)):
            act(copy)
        if not halves:
            for copy in copies(outer_at, (outer_hbm,), (3,)):
                act(copy)
            return
        is_bent = (row_idx == bent[0]) | (row_idx == bent[1])

        @pl.when(jnp.logical_not(is_bent))
        def _():
            for copy in copies(outer_at, (outer_hbm,), (3,)):
                act(copy)

        @pl.when(is_bent)
        def _():
            for copy in copies(outer_at, halves, (3, 4)):
                act(copy)

    all_copies(lambda copy: copy.start())
    all_copies(lambda copy: copy.wait())
    tile = min(256, half)
    odd = lax.rem(col_idx, 2)
    for i in range(rows):
        lhs = jnp.concatenate([f_ref[i, e] for e in range(STENCIL)], axis=1)
        starts = [
            pl.multiple_of((cols_ref[e, base + i] - base + BAND) * bs, bs)
            for e in range(STENCIL)
        ]
        for part, out_ref in ((1 - odd, first_ref), (odd, second_ref)):
            for t in range(half // tile):
                at = pl.ds(pl.multiple_of(part * half + t * tile, bs), tile)
                rhs = jnp.concatenate([ext[pl.ds(s, bs), at] for s in starts], axis=0)
                out_ref[i * bs : (i + 1) * bs, t * tile : (t + 1) * tile] = jnp.dot(
                    lhs, rhs, preferred_element_type=jnp.float32
                ).astype(out_ref.dtype)


def stage2_kernel(fan, turn, cols_ref, mask_ref, q_ref, w_ref, f_ref, *refs):
    if turn == 0:
        *parts, out_hbm, ext, made, out_sem, sem = refs
    else:
        ext, _, out_hbm, made, out_sem = refs
        parts = []
    group, bs = f_ref.shape[0], f_ref.shape[2]
    rows, slab = mask_ref.shape
    row_idx, col_idx = lax.axis_index("row"), lax.axis_index("col")
    base = lax.rem(row_idx + turn, fan) * group
    first = col_idx * slab - BAND

    joins = []
    odd = lax.rem(col_idx, 2)
    for piece, part in enumerate(parts):
        width = part.shape[1]
        at = odd * piece + (1 - odd) * (len(parts) - 1 - piece)
        to = ext.at[:, pl.ds(pl.multiple_of(at * width, width), width)]
        joins.append(pltpu.make_async_copy(part, to, sem.at[piece]))
    for copy in joins:
        copy.start()
    for copy in joins:
        copy.wait()

    eye = lax.broadcasted_iota(jnp.int32, (bs, bs), 0) == lax.broadcasted_iota(
        jnp.int32, (bs, bs), 1
    )
    stores = []
    for n in range(group):
        j = base + n
        col = col_idx * slab + j
        to = pl.ds(pl.multiple_of(j * bs, bs), bs)
        lhs = jnp.concatenate(
            [
                ext[:, pl.ds(pl.multiple_of((cols_ref[e, col] - first) * bs, bs), bs)]
                for e in range(STENCIL)
            ],
            axis=1,
        )
        rhs = jnp.concatenate([f_ref[n, e] for e in range(STENCIL)], axis=1)
        spread = lax.dot_general(
            lhs, rhs, (((1,), (1,)), ((), ())), preferred_element_type=jnp.float32
        )
        for i in range(rows):
            at = slice(i * bs, (i + 1) * bs)
            keep = mask_ref[i, j].astype(jnp.float32)
            on_main = (row_idx * rows + i == col).astype(jnp.float32)
            noise = jnp.where(eye, q_ref[i : i + 1, :] * on_main, 0.0)
            made[n, at, :] = w_ref[at, to].astype(jnp.float32) * (spread[at] * keep) + noise
        store = pltpu.make_async_copy(made.at[n], out_hbm.at[:, to], out_sem.at[n])
        store.start()
        stores.append(store)
    for store in stores:
        store.wait()


def forecast(
    p_cov, f_blocks, stencil_cols, localization_weights, block_mask, disturbance_variances
):
    rows, cols = lax.axis_size("row"), lax.axis_size("col")
    fan = rows // cols
    block_rows, bs = f_blocks.shape[0], f_blocks.shape[2]
    tall, wide = p_cov.shape
    slab = wide // bs
    halo = BAND * bs
    assert tall == halo and wide == 2 * halo
    cols_of = stencil_cols.T

    smem = pl.BlockSpec(memory_space=pltpu.SMEM)
    hbm = pl.BlockSpec(memory_space=ANY)
    vmem = pl.BlockSpec(memory_space=pltpu.VMEM)
    top, bottom = p_cov[: tall // 2], p_cov[tall // 2 :]
    f_near, cols_of = pl.pallas_call(
        fetch_kernel,
        out_shape=tuple(jax.ShapeDtypeStruct(x.shape, x.dtype) for x in (f_blocks, cols_of)),
        in_specs=[hbm, hbm],
        out_specs=(vmem, vmem),
        scratch_shapes=[pltpu.SemaphoreType.DMA((2,))],
        compiler_params=pltpu.CompilerParams(vmem_limit_bytes=8 * 2**20),
        name="fetch",
    )(f_blocks, cols_of)

    inner_pairs, outer_pairs = exchanges(rows)
    bent, halves = (rows // 2, rows // 2 - 1), ()
    if (cols, fan) == (4, 2):
        lower, upper = bent
        across = [(upper, lower), (lower, upper)]
        outer_pairs = [pair for pair in outer_pairs if pair not in across]
        straight = lax.ppermute(top, "row", across)
        turn = lax.ppermute(bottom, "row", [(upper, rows - 1), (lower, 0)])
        turned = lax.ppermute(turn, "row", [(rows - 1, lower), (0, upper)])
        halves = (straight, turned)
    inner = lax.ppermute(p_cov, "row", inner_pairs)
    outer = lax.ppermute(p_cov, "row", outer_pairs)
    held = [f_blocks]
    for source, pairs in group_plan(rows, cols):
        held.append(lax.ppermute(held[source], ("row", "col"), pairs))

    half = jax.ShapeDtypeStruct((tall, halo), jnp.bfloat16)
    first, second = pl.pallas_call(
        functools.partial(stage1_kernel, bent),
        out_shape=(half, half),
        in_specs=[smem, vmem] + [hbm] * (4 + len(halves)),
        out_specs=(vmem, vmem),
        scratch_shapes=[
            pltpu.VMEM((tall + 2 * halo, wide), jnp.bfloat16),
            pltpu.SemaphoreType.DMA((5,)),
        ],
        compiler_params=pltpu.CompilerParams(vmem_limit_bytes=16 * 2**20),
        name="stage1",
    )(cols_of, f_near, top, bottom, inner, outer, *halves)

    inner_pairs, outer_pairs = exchanges(cols)
    nearer = lax.ppermute(first, "col", inner_pairs)
    further = lax.ppermute(second, "col", outer_pairs)

    mine = pl.pallas_call(
        functools.partial(pick_kernel, holder_table(rows, cols)),
        out_shape=jax.ShapeDtypeStruct(f_blocks.shape, f_blocks.dtype),
        in_specs=[hbm] * len(held),
        out_specs=vmem,
        scratch_shapes=[pltpu.SemaphoreType.DMA],
        compiler_params=pltpu.CompilerParams(vmem_limit_bytes=4 * 2**20),
        name="pick",
    )(*held)
    fixed = (
        cols_of,
        block_mask,
        disturbance_variances.reshape(block_rows, bs),
        localization_weights,
    )
    out_type = jax.ShapeDtypeStruct((tall, wide), jnp.float32)
    group = slab // fan
    scratch = [
        pltpu.VMEM((group, tall, bs), jnp.float32),
        pltpu.SemaphoreType.DMA((group,)),
    ]
    params = pltpu.CompilerParams(vmem_limit_bytes=20 * 2**20)
    out, ext = pl.pallas_call(
        functools.partial(stage2_kernel, fan, 0),
        out_shape=(out_type, jax.ShapeDtypeStruct((tall, wide + 2 * halo), jnp.bfloat16)),
        in_specs=[smem, smem, vmem, vmem, vmem] + [hbm] * 4,
        out_specs=(pl.BlockSpec(memory_space=pltpu.HBM), vmem),
        scratch_shapes=scratch + [pltpu.SemaphoreType.DMA((4,))],
        compiler_params=params,
        name="stage2",
    )(*fixed, mine, nearer, first, second, further)
    for turn in range(1, fan):
        pairs = [(r // fan * fan + (r + turn) % fan, r) for r in range(rows)]
        other = lax.ppermute(mine, "row", pairs)
        out = pl.pallas_call(
            functools.partial(stage2_kernel, fan, turn),
            out_shape=out_type,
            in_specs=[smem, smem, vmem, vmem, vmem, vmem, pl.BlockSpec(memory_space=pltpu.HBM)],
            out_specs=pl.BlockSpec(memory_space=pltpu.HBM),
            scratch_shapes=scratch,
            input_output_aliases={6: 0},
            compiler_params=params,
            name="stage3",
        )(*fixed, other, ext, out)
    return out


def solution(mesh):
    placed = (
        P("row", "col"),
        P("row", None, None, None),
        P(),
        P("row", "col"),
        P("row", "col"),
        P("row"),
    )
    return jax.shard_map(
        forecast, mesh=mesh, in_specs=placed, out_specs=P("row", "col"), check_vma=False
    )
```

```python
import functools

import jax
import jax.numpy as jnp
from jax import lax
from jax.experimental import pallas as pl
from jax.experimental.pallas import tpu as pltpu
from jax.sharding import PartitionSpec as P


STENCIL = 7
BAND = 4
ANY = pl.ANY


def exchanges(devices):
    both = []
    for start in (0, 1):
        pairs = [(i, i + 1) for i in range(start, devices - 1, 2)]
        both.append(pairs + [(j, i) for i, j in pairs])
    return both


def source_plane(c, a, cols):
    if cols & (cols - 1):
        return a
    return c ^ (((a ^ c) - 1) % cols)


def group_plan(rows, cols):
    fan = rows // cols

    def at(a, k, c):
        return (a * fan + k) * cols + c

    if not relayed(rows, cols):
        pairs = []
        for c in range(cols):
            for a in range(cols):
                if a != c:
                    plane = source_plane(c, a, cols)
                    pairs += [(at(c, k, plane), at(a, k, c)) for k in range(fan)]
        return [pairs]
    first, second = [], []
    for c in range(cols):
        near, side, far = c ^ 1, c ^ 2, c ^ 3
        first += [(at(c, 0, c), at(near, 0, c)), (at(c, 1, c), at(side, 1, c))]
        second += [
            (at(near, 0, c), at(far, 0, c)),
            (at(side, 1, c), at(far, 1, c)),
            (at(c, 0, c), at(side, 0, c)),
            (at(c, 1, c), at(near, 1, c)),
        ]
    return [first, second]


def relayed(rows, cols):
    return (rows, cols) == (8, 4)


def held_early(row, col, rows, cols):
    fan = rows // cols
    if isinstance(row, int):
        chip, core = divmod(row, fan)
    else:
        chip, core = lax.div(row, fan), lax.rem(row, fan)
    if not relayed(rows, cols):
        return chip == col
    way = chip ^ col
    return (way == 0) | ((way == 1) & (core == 0)) | ((way == 2) & (core == 1))


def pick_kernel(fan, own_hbm, got_hbm, out_ref, sem):
    own = lax.div(lax.axis_index("row"), fan) == lax.axis_index("col")
    for source, wanted in ((own_hbm, own), (got_hbm, jnp.logical_not(own))):

        @pl.when(wanted)
        def _():
            copies = [
                pltpu.make_async_copy(source.at[n], out_ref.at[n], sem.at[n])
                for n in range(out_ref.shape[0])
            ]
            for copy in copies:
                copy.start()
            for copy in copies:
                copy.wait()


def fetch_kernel(f_hbm, cols_hbm, f_ref, cols_ref, sem):
    copies = [
        pltpu.make_async_copy(f_hbm, f_ref, sem.at[0]),
        pltpu.make_async_copy(cols_hbm, cols_ref, sem.at[1]),
    ]
    for copy in copies:
        copy.start()
    for copy in copies:
        copy.wait()


def stage1_kernel(bent, cols_ref, f_ref, top_hbm, bottom_hbm, inner_hbm, outer_hbm, *refs):
    *halves, first_ref, second_ref, ext, sem = refs
    rows, bs = f_ref.shape[0], f_ref.shape[2]
    half = first_ref.shape[1]
    row_idx, col_idx = lax.axis_index("row"), lax.axis_index("col")
    base = row_idx * rows
    halo, part = inner_hbm.shape[0], top_hbm.shape[0]
    below = halo + 2 * part
    odd = lax.rem(row_idx, 2)
    inner_at = pl.multiple_of((1 - odd) * below, bs)
    outer_at = pl.multiple_of(odd * below, bs)

    def copies(at, pieces, sems):
        for piece, n in zip(pieces, sems):
            yield pltpu.make_async_copy(piece, ext.at[pl.ds(at, piece.shape[0])], sem.at[n])
            at += piece.shape[0]

    def all_copies(act):
        for copy in copies(halo, (top_hbm, bottom_hbm), (0, 1)):
            act(copy)
        for copy in copies(inner_at, (inner_hbm,), (2,)):
            act(copy)
        if not halves:
            for copy in copies(outer_at, (outer_hbm,), (3,)):
                act(copy)
            return
        is_bent = (row_idx == bent[0]) | (row_idx == bent[1])

        @pl.when(jnp.logical_not(is_bent))
        def _():
            for copy in copies(outer_at, (outer_hbm,), (3,)):
                act(copy)

        @pl.when(is_bent)
        def _():
            for copy in copies(outer_at, halves, (3, 4)):
                act(copy)

    all_copies(lambda copy: copy.start())
    all_copies(lambda copy: copy.wait())
    tile = min(256, half)
    odd = lax.rem(col_idx, 2)
    for i in range(rows):
        lhs = jnp.concatenate([f_ref[i, e] for e in range(STENCIL)], axis=1)
        starts = [
            pl.multiple_of((cols_ref[e, base + i] - base + BAND) * bs, bs)
            for e in range(STENCIL)
        ]
        for part, out_ref in ((1 - odd, first_ref), (odd, second_ref)):
            for t in range(half // tile):
                at = pl.ds(pl.multiple_of(part * half + t * tile, bs), tile)
                rhs = jnp.concatenate([ext[pl.ds(s, bs), at] for s in starts], axis=0)
                out_ref[i * bs : (i + 1) * bs, t * tile : (t + 1) * tile] = jnp.dot(
                    lhs, rhs, preferred_element_type=jnp.float32
                ).astype(out_ref.dtype)


def stage2_kernel(
    sizes, turn, cols_ref, mask_ref, q_ref, w_ref, early_ref, late_ref, *refs
):
    fan = sizes[0] // sizes[1]
    ready = []
    if turn == 0:
        *parts, made, ext, sem = refs
    else:
        ext, *ready = refs[:-4] if turn == fan - 1 else refs[:-1]
        parts = []
        if turn == fan - 1:
            out_hbm, made, out_sem, ready_sem = refs[-4:]
        else:
            made = refs[-1]
    group, bs = early_ref.shape[0], early_ref.shape[2]
    rows, slab = mask_ref.shape
    row_idx, col_idx = lax.axis_index("row"), lax.axis_index("col")
    first = col_idx * slab - BAND
    core = lax.rem(row_idx, fan)
    owner = row_idx - core + lax.rem(core + turn, fan)
    early = held_early(owner, col_idx, *sizes)

    def column(turn, n):
        return lax.rem(row_idx + turn, fan) * group + n

    def place(j):
        return pl.ds(pl.multiple_of(j * bs, bs), bs)

    stores = []
    for before, done in enumerate(ready):
        for n in range(group):
            to = out_hbm.at[:, place(column(before, n))]
            stores.append(pltpu.make_async_copy(done.at[n], to, ready_sem.at[before, n]))
    joins = []
    odd = lax.rem(col_idx, 2)
    for piece, part in enumerate(parts):
        width = part.shape[1]
        at = odd * piece + (1 - odd) * (len(parts) - 1 - piece)
        to = ext.at[:, pl.ds(pl.multiple_of(at * width, width), width)]
        joins.append(pltpu.make_async_copy(part, to, sem.at[piece]))
    for copy in joins + stores:
        copy.start()
    for copy in joins:
        copy.wait()

    eye = lax.broadcasted_iota(jnp.int32, (bs, bs), 0) == lax.broadcasted_iota(
        jnp.int32, (bs, bs), 1
    )
    for n in range(group):
        j = column(turn, n)
        col = col_idx * slab + j
        to = place(j)
        lhs = jnp.concatenate(
            [
                ext[:, pl.ds(pl.multiple_of((cols_ref[e, col] - first) * bs, bs), bs)]
                for e in range(STENCIL)
            ],
            axis=1,
        )
        rhs = jnp.concatenate(
            [jnp.where(early, early_ref[n, e], late_ref[n, e]) for e in range(STENCIL)], axis=1
        )
        spread = lax.dot_general(
            lhs, rhs, (((1,), (1,)), ((), ())), preferred_element_type=jnp.float32
        )
        for i in range(rows):
            at = slice(i * bs, (i + 1) * bs)
            keep = mask_ref[i, j].astype(jnp.float32)
            on_main = (row_idx * rows + i == col).astype(jnp.float32)
            noise = jnp.where(eye, q_ref[i : i + 1, :] * on_main, 0.0)
            made[n, at, :] = w_ref[at, to].astype(jnp.float32) * (spread[at] * keep) + noise
        if turn == fan - 1:
            store = pltpu.make_async_copy(made.at[n], out_hbm.at[:, to], out_sem.at[n])
            store.start()
            stores.append(store)
    for store in stores:
        store.wait()


def forecast(
    p_cov, f_blocks, stencil_cols, localization_weights, block_mask, disturbance_variances
):
    rows, cols = lax.axis_size("row"), lax.axis_size("col")
    fan = rows // cols
    block_rows, bs = f_blocks.shape[0], f_blocks.shape[2]
    tall, wide = p_cov.shape
    slab = wide // bs
    halo = BAND * bs
    assert tall == halo and wide == 2 * halo
    cols_of = stencil_cols.T

    smem = pl.BlockSpec(memory_space=pltpu.SMEM)
    hbm = pl.BlockSpec(memory_space=ANY)
    vmem = pl.BlockSpec(memory_space=pltpu.VMEM)
    top, bottom = p_cov[: tall // 2], p_cov[tall // 2 :]
    f_near, cols_of = pl.pallas_call(
        fetch_kernel,
        out_shape=tuple(jax.ShapeDtypeStruct(x.shape, x.dtype) for x in (f_blocks, cols_of)),
        in_specs=[hbm, hbm],
        out_specs=(vmem, vmem),
        scratch_shapes=[pltpu.SemaphoreType.DMA((2,))],
        compiler_params=pltpu.CompilerParams(vmem_limit_bytes=8 * 2**20),
        name="fetch",
    )(f_blocks, cols_of)

    inner_pairs, outer_pairs = exchanges(rows)
    bent, halves = (rows // 2, rows // 2 - 1), ()
    if (cols, fan) == (4, 2):
        lower, upper = bent
        across = [(upper, lower), (lower, upper)]
        outer_pairs = [pair for pair in outer_pairs if pair not in across]
        straight = lax.ppermute(top, "row", across)
        turn = lax.ppermute(bottom, "row", [(upper, rows - 1), (lower, 0)])
        turned = lax.ppermute(turn, "row", [(rows - 1, lower), (0, upper)])
        halves = (straight, turned)
    inner = lax.ppermute(p_cov, "row", inner_pairs)
    outer = lax.ppermute(p_cov, "row", outer_pairs)
    plan = group_plan(rows, cols)
    early, late = f_blocks, lax.ppermute(f_blocks, ("row", "col"), plan[0])
    if len(plan) > 1:
        early = pl.pallas_call(
            functools.partial(pick_kernel, fan),
            out_shape=jax.ShapeDtypeStruct(f_blocks.shape, f_blocks.dtype),
            in_specs=[hbm, hbm],
            out_specs=vmem,
            scratch_shapes=[pltpu.SemaphoreType.DMA((block_rows,))],
            compiler_params=pltpu.CompilerParams(vmem_limit_bytes=4 * 2**20),
            name="pick",
        )(f_blocks, late)
        late = lax.ppermute(early, ("row", "col"), plan[1])
    half = jax.ShapeDtypeStruct((tall, halo), jnp.bfloat16)
    first, second = pl.pallas_call(
        functools.partial(stage1_kernel, bent),
        out_shape=(half, half),
        in_specs=[smem, vmem] + [hbm] * (4 + len(halves)),
        out_specs=(vmem, vmem),
        scratch_shapes=[
            pltpu.VMEM((tall + 2 * halo, wide), jnp.bfloat16),
            pltpu.SemaphoreType.DMA((5,)),
        ],
        compiler_params=pltpu.CompilerParams(vmem_limit_bytes=16 * 2**20),
        name="stage1",
    )(cols_of, f_near, top, bottom, inner, outer, *halves)

    inner_pairs, outer_pairs = exchanges(cols)
    nearer = lax.ppermute(first, "col", inner_pairs)
    further = lax.ppermute(second, "col", outer_pairs)

    fixed = (
        cols_of,
        block_mask,
        disturbance_variances.reshape(block_rows, bs),
        localization_weights,
    )
    assert fan > 1
    group = slab // fan
    made_type = jax.ShapeDtypeStruct((group, tall, bs), jnp.float32)
    params = pltpu.CompilerParams(vmem_limit_bytes=20 * 2**20)
    made, ext = pl.pallas_call(
        functools.partial(stage2_kernel, (rows, cols), 0),
        out_shape=(made_type, jax.ShapeDtypeStruct((tall, wide + 2 * halo), jnp.bfloat16)),
        in_specs=[smem, smem] + [vmem] * 4 + [hbm] * 4,
        out_specs=(vmem, vmem),
        scratch_shapes=[pltpu.SemaphoreType.DMA((4,))],
        compiler_params=params,
        name="stage2",
    )(*fixed, early, late, nearer, first, second, further)
    ready = [made]
    for turn in range(1, fan):
        last = turn == fan - 1
        pairs = {True: [], False: []}
        for r in range(rows):
            source = r // fan * fan + (r + turn) % fan
            for c in range(cols):
                pair = (source * cols + c, r * cols + c)
                pairs[held_early(source, c, rows, cols)].append(pair)
        sent_early = lax.ppermute(early, ("row", "col"), pairs[True])
        sent_late = lax.ppermute(late, ("row", "col"), pairs[False])
        ready.append(
            pl.pallas_call(
                functools.partial(stage2_kernel, (rows, cols), turn),
                out_shape=jax.ShapeDtypeStruct((tall, wide), jnp.float32) if last else made_type,
                in_specs=[smem, smem] + [vmem] * (5 + len(ready) * last),
                out_specs=pl.BlockSpec(memory_space=pltpu.HBM) if last else vmem,
                scratch_shapes=[
                    pltpu.VMEM(made_type.shape, made_type.dtype),
                    pltpu.SemaphoreType.DMA((group,)),
                    pltpu.SemaphoreType.DMA((turn, group)),
                ]
                * last,
                compiler_params=params,
                name="stage3",
            )(*fixed, sent_early, sent_late, ext, *(ready * last))
        )
    return ready[-1]


def solution(mesh):
    placed = (
        P("row", "col"),
        P("row", None, None, None),
        P(),
        P("row", "col"),
        P("row", "col"),
        P("row"),
    )
    return jax.shard_map(
        forecast, mesh=mesh, in_specs=placed, out_specs=P("row", "col"), check_vma=False
    )
```

```python
import functools

import jax
import jax.numpy as jnp
from jax import lax
from jax.experimental import pallas as pl
from jax.experimental.pallas import tpu as pltpu
from jax.sharding import PartitionSpec as P


STENCIL = 7
BAND = 4
ANY = pl.ANY


def exchanges(devices):
    both = []
    for start in (0, 1):
        pairs = [(i, i + 1) for i in range(start, devices - 1, 2)]
        both.append(pairs + [(j, i) for i, j in pairs])
    return both


def source_plane(c, a, cols):
    if cols & (cols - 1):
        return a
    return c ^ (((a ^ c) - 1) % cols)


def group_plan(rows, cols):
    fan = rows // cols

    def at(a, k, c):
        return (a * fan + k) * cols + c

    if (cols, fan) != (4, 2):
        pairs = []
        for c in range(cols):
            for a in range(cols):
                if a != c:
                    plane = source_plane(c, a, cols)
                    pairs += [(at(c, k, plane), at(a, k, c)) for k in range(fan)]
        return [(0, pairs)]
    first, relayed, second = [], [], []
    for c in range(cols):
        near, side, far = c ^ 1, c ^ 2, c ^ 3
        i, j = (1, 0) if c in (1, 2) else (0, 1)
        first += [(at(c, i, c), at(near, i, c)), (at(c, j, c), at(side, j, c))]
        relayed += [(at(near, i, c), at(far, i, c)), (at(side, j, c), at(far, j, c))]
        second += [(at(c, i, c), at(side, i, c)), (at(c, j, c), at(near, j, c))]
    return [(0, first), (1, relayed), (0, second)]


def holder_table(rows, cols):
    table = [0] * (rows * cols)
    for step, (_, pairs) in enumerate(group_plan(rows, cols)):
        for _, target in pairs:
            table[target] = step + 1
    return table


def pick_kernel(table, *refs):
    *sources, out_ref, sem = refs
    me = lax.axis_index("row") * lax.axis_size("col") + lax.axis_index("col")
    which = 0
    for device, step in enumerate(table):
        if step:
            which = jnp.where(me == device, step, which)
    for step, source in enumerate(sources):

        @pl.when(which == step)
        def _():
            copies = [
                pltpu.make_async_copy(source.at[n], out_ref.at[n], sem.at[n])
                for n in range(out_ref.shape[0])
            ]
            for copy in copies:
                copy.start()
            for copy in copies:
                copy.wait()


def fetch_kernel(f_hbm, cols_hbm, f_ref, cols_ref, sem):
    copies = [
        pltpu.make_async_copy(f_hbm, f_ref, sem.at[0]),
        pltpu.make_async_copy(cols_hbm, cols_ref, sem.at[1]),
    ]
    for copy in copies:
        copy.start()
    for copy in copies:
        copy.wait()


def stage1_kernel(bent, cols_ref, f_ref, top_hbm, bottom_hbm, inner_hbm, outer_hbm, *refs):
    *halves, first_ref, second_ref, ext, sem = refs
    rows, bs = f_ref.shape[0], f_ref.shape[2]
    half = first_ref.shape[1]
    row_idx, col_idx = lax.axis_index("row"), lax.axis_index("col")
    base = row_idx * rows
    halo, part = inner_hbm.shape[0], top_hbm.shape[0]
    below = halo + 2 * part
    odd = lax.rem(row_idx, 2)
    inner_at = pl.multiple_of((1 - odd) * below, bs)
    outer_at = pl.multiple_of(odd * below, bs)

    def copies(at, pieces, sems):
        for piece, n in zip(pieces, sems):
            yield pltpu.make_async_copy(piece, ext.at[pl.ds(at, piece.shape[0])], sem.at[n])
            at += piece.shape[0]

    def all_copies(act):
        for copy in copies(halo, (top_hbm, bottom_hbm), (0, 1)):
            act(copy)
        for copy in copies(inner_at, (inner_hbm,), (2,)):
            act(copy)
        if not halves:
            for copy in copies(outer_at, (outer_hbm,), (3,)):
                act(copy)
            return
        is_bent = (row_idx == bent[0]) | (row_idx == bent[1])

        @pl.when(jnp.logical_not(is_bent))
        def _():
            for copy in copies(outer_at, (outer_hbm,), (3,)):
                act(copy)

        @pl.when(is_bent)
        def _():
            for copy in copies(outer_at, halves, (3, 4)):
                act(copy)

    all_copies(lambda copy: copy.start())
    all_copies(lambda copy: copy.wait())
    tile = min(256, half)
    odd = lax.rem(col_idx, 2)
    for i in range(rows):
        lhs = jnp.concatenate([f_ref[i, e] for e in range(STENCIL)], axis=1)
        starts = [
            pl.multiple_of((cols_ref[e, base + i] - base + BAND) * bs, bs)
            for e in range(STENCIL)
        ]
        for part, out_ref in ((1 - odd, first_ref), (odd, second_ref)):
            for t in range(half // tile):
                at = pl.ds(pl.multiple_of(part * half + t * tile, bs), tile)
                rhs = jnp.concatenate([ext[pl.ds(s, bs), at] for s in starts], axis=0)
                out_ref[i * bs : (i + 1) * bs, t * tile : (t + 1) * tile] = jnp.dot(
                    lhs, rhs, preferred_element_type=jnp.float32
                ).astype(out_ref.dtype)


def stage2_kernel(fan, turn, cols_ref, mask_ref, q_ref, w_ref, f_ref, *refs):
    ready = []
    if turn == 0:
        *parts, made, ext, sem = refs
    else:
        ext, *ready = refs[:-4] if turn == fan - 1 else refs[:-1]
        parts = []
        if turn == fan - 1:
            out_hbm, made, out_sem, ready_sem = refs[-4:]
        else:
            made = refs[-1]
    group, bs = f_ref.shape[0], f_ref.shape[2]
    rows, slab = mask_ref.shape
    row_idx, col_idx = lax.axis_index("row"), lax.axis_index("col")
    first = col_idx * slab - BAND

    def column(turn, n):
        return lax.rem(row_idx + turn, fan) * group + n

    def place(j):
        return pl.ds(pl.multiple_of(j * bs, bs), bs)

    stores = []
    for before, done in enumerate(ready):
        for n in range(group):
            to = out_hbm.at[:, place(column(before, n))]
            stores.append(pltpu.make_async_copy(done.at[n], to, ready_sem.at[before, n]))
    joins = []
    odd = lax.rem(col_idx, 2)
    for piece, part in enumerate(parts):
        width = part.shape[1]
        at = odd * piece + (1 - odd) * (len(parts) - 1 - piece)
        to = ext.at[:, pl.ds(pl.multiple_of(at * width, width), width)]
        joins.append(pltpu.make_async_copy(part, to, sem.at[piece]))
    for copy in joins + stores:
        copy.start()
    for copy in joins:
        copy.wait()

    eye = lax.broadcasted_iota(jnp.int32, (bs, bs), 0) == lax.broadcasted_iota(
        jnp.int32, (bs, bs), 1
    )
    for n in range(group):
        j = column(turn, n)
        col = col_idx * slab + j
        to = place(j)
        lhs = jnp.concatenate(
            [
                ext[:, pl.ds(pl.multiple_of((cols_ref[e, col] - first) * bs, bs), bs)]
                for e in range(STENCIL)
            ],
            axis=1,
        )
        rhs = jnp.concatenate([f_ref[n, e] for e in range(STENCIL)], axis=1)
        spread = lax.dot_general(
            lhs, rhs, (((1,), (1,)), ((), ())), preferred_element_type=jnp.float32
        )
        for i in range(rows):
            at = slice(i * bs, (i + 1) * bs)
            keep = mask_ref[i, j].astype(jnp.float32)
            on_main = (row_idx * rows + i == col).astype(jnp.float32)
            noise = jnp.where(eye, q_ref[i : i + 1, :] * on_main, 0.0)
            made[n, at, :] = w_ref[at, to].astype(jnp.float32) * (spread[at] * keep) + noise
        if turn == fan - 1:
            store = pltpu.make_async_copy(made.at[n], out_hbm.at[:, to], out_sem.at[n])
            store.start()
            stores.append(store)
    for store in stores:
        store.wait()


def forecast(
    p_cov, f_blocks, stencil_cols, localization_weights, block_mask, disturbance_variances
):
    rows, cols = lax.axis_size("row"), lax.axis_size("col")
    fan = rows // cols
    block_rows, bs = f_blocks.shape[0], f_blocks.shape[2]
    tall, wide = p_cov.shape
    slab = wide // bs
    halo = BAND * bs
    assert tall == halo and wide == 2 * halo
    cols_of = stencil_cols.T

    smem = pl.BlockSpec(memory_space=pltpu.SMEM)
    hbm = pl.BlockSpec(memory_space=ANY)
    vmem = pl.BlockSpec(memory_space=pltpu.VMEM)
    top, bottom = p_cov[: tall // 2], p_cov[tall // 2 :]
    f_near, cols_of = pl.pallas_call(
        fetch_kernel,
        out_shape=tuple(jax.ShapeDtypeStruct(x.shape, x.dtype) for x in (f_blocks, cols_of)),
        in_specs=[hbm, hbm],
        out_specs=(vmem, vmem),
        scratch_shapes=[pltpu.SemaphoreType.DMA((2,))],
        compiler_params=pltpu.CompilerParams(vmem_limit_bytes=8 * 2**20),
        name="fetch",
    )(f_blocks, cols_of)

    inner_pairs, outer_pairs = exchanges(rows)
    bent, halves = (rows // 2, rows // 2 - 1), ()
    if (cols, fan) == (4, 2):
        lower, upper = bent
        across = [(upper, lower), (lower, upper)]
        outer_pairs = [pair for pair in outer_pairs if pair not in across]
        straight = lax.ppermute(top, "row", across)
        turn = lax.ppermute(bottom, "row", [(upper, rows - 1), (lower, 0)])
        turned = lax.ppermute(turn, "row", [(rows - 1, lower), (0, upper)])
        halves = (straight, turned)
    inner = lax.ppermute(p_cov, "row", inner_pairs)
    outer = lax.ppermute(p_cov, "row", outer_pairs)
    held = [f_blocks]
    for source, pairs in group_plan(rows, cols):
        held.append(lax.ppermute(held[source], ("row", "col"), pairs))

    half = jax.ShapeDtypeStruct((tall, halo), jnp.bfloat16)
    first, second = pl.pallas_call(
        functools.partial(stage1_kernel, bent),
        out_shape=(half, half),
        in_specs=[smem, vmem] + [hbm] * (4 + len(halves)),
        out_specs=(vmem, vmem),
        scratch_shapes=[
            pltpu.VMEM((tall + 2 * halo, wide), jnp.bfloat16),
            pltpu.SemaphoreType.DMA((5,)),
        ],
        compiler_params=pltpu.CompilerParams(vmem_limit_bytes=16 * 2**20),
        name="stage1",
    )(cols_of, f_near, top, bottom, inner, outer, *halves)

    inner_pairs, outer_pairs = exchanges(cols)
    idle = set(range(cols)) - {i for i, _ in outer_pairs}
    outer_pairs = outer_pairs + [(i, i) for i in sorted(idle)]
    nearer = lax.ppermute(first, "col", inner_pairs)
    further = lax.ppermute(second, "col", outer_pairs)

    mine = pl.pallas_call(
        functools.partial(pick_kernel, holder_table(rows, cols)),
        out_shape=jax.ShapeDtypeStruct(f_blocks.shape, f_blocks.dtype),
        in_specs=[vmem] * len(held),
        out_specs=vmem,
        scratch_shapes=[pltpu.SemaphoreType.DMA((block_rows,))],
        compiler_params=pltpu.CompilerParams(vmem_limit_bytes=4 * 2**20),
        name="pick",
    )(*held)
    fixed = (
        cols_of,
        block_mask,
        disturbance_variances.reshape(block_rows, bs),
        localization_weights,
    )
    assert fan > 1
    group = slab // fan
    made_type = jax.ShapeDtypeStruct((group, tall, bs), jnp.float32)
    params = pltpu.CompilerParams(vmem_limit_bytes=20 * 2**20)
    made, ext = pl.pallas_call(
        functools.partial(stage2_kernel, fan, 0),
        out_shape=(made_type, jax.ShapeDtypeStruct((tall, wide + 2 * halo), jnp.bfloat16)),
        in_specs=[smem, smem, vmem, vmem, vmem] + [hbm] * 4,
        out_specs=(vmem, vmem),
        scratch_shapes=[pltpu.SemaphoreType.DMA((4,))],
        compiler_params=params,
        name="stage2",
    )(*fixed, mine, nearer, first, second, further)
    ready = [made]
    for turn in range(1, fan):
        last = turn == fan - 1
        pairs = [(r // fan * fan + (r + turn) % fan, r) for r in range(rows)]
        other = lax.ppermute(mine, "row", pairs)
        ready.append(
            pl.pallas_call(
                functools.partial(stage2_kernel, fan, turn),
                out_shape=jax.ShapeDtypeStruct((tall, wide), jnp.float32) if last else made_type,
                in_specs=[smem, smem, vmem, vmem, vmem, vmem] + [vmem] * (len(ready) * last),
                out_specs=pl.BlockSpec(memory_space=pltpu.HBM) if last else vmem,
                scratch_shapes=[
                    pltpu.VMEM(made_type.shape, made_type.dtype),
                    pltpu.SemaphoreType.DMA((group,)),
                    pltpu.SemaphoreType.DMA((turn, group)),
                ]
                * last,
                compiler_params=params,
                name="stage3",
            )(*fixed, other, ext, *(ready * last))
        )
    return ready[-1]


def solution(mesh):
    placed = (
        P("row", "col"),
        P("row", None, None, None),
        P(),
        P("row", "col"),
        P("row", "col"),
        P("row"),
    )
    return jax.shard_map(
        forecast, mesh=mesh, in_specs=placed, out_specs=P("row", "col"), check_vma=False
    )
```

```python
import functools

import jax
import jax.numpy as jnp
from jax import lax
from jax.experimental import pallas as pl
from jax.experimental.pallas import tpu as pltpu
from jax.sharding import PartitionSpec as P


STENCIL = 7
BAND = 4
ANY = pl.ANY


def exchanges(devices):
    both = []
    for start in (0, 1):
        pairs = [(i, i + 1) for i in range(start, devices - 1, 2)]
        both.append(pairs + [(j, i) for i, j in pairs])
    return both


def source_plane(c, a, cols):
    if cols & (cols - 1):
        return a
    return c ^ (((a ^ c) - 1) % cols)


def group_plan(rows, cols):
    fan = rows // cols

    def at(a, k, c):
        return (a * fan + k) * cols + c

    if (cols, fan) != (4, 2):
        pairs = []
        for c in range(cols):
            for a in range(cols):
                if a != c:
                    plane = source_plane(c, a, cols)
                    pairs += [(at(c, k, plane), at(a, k, c)) for k in range(fan)]
        return [(0, pairs)]
    first, relayed, second = [], [], []
    for c in range(cols):
        near, side, far = c ^ 1, c ^ 2, c ^ 3
        first += [(at(c, 0, c), at(near, 0, c)), (at(c, 1, c), at(side, 1, c))]
        relayed += [(at(near, 0, c), at(far, 0, c)), (at(side, 1, c), at(far, 1, c))]
        second += [(at(c, 0, c), at(side, 0, c)), (at(c, 1, c), at(near, 1, c))]
    return [(0, first), (1, relayed), (0, second)]


def holder_table(rows, cols):
    table = [0] * (rows * cols)
    for step, (_, pairs) in enumerate(group_plan(rows, cols)):
        for _, target in pairs:
            table[target] = step + 1
    return table


def pick_kernel(table, *refs):
    *sources, out_ref, sem = refs
    me = lax.axis_index("row") * lax.axis_size("col") + lax.axis_index("col")
    which = 0
    for device, step in enumerate(table):
        if step:
            which = jnp.where(me == device, step, which)
    for step, source in enumerate(sources):

        @pl.when(which == step)
        def _():
            copies = [
                pltpu.make_async_copy(source.at[n], out_ref.at[n], sem.at[n])
                for n in range(out_ref.shape[0])
            ]
            for copy in copies:
                copy.start()
            for copy in copies:
                copy.wait()


def fetch_kernel(f_hbm, cols_hbm, f_ref, cols_ref, sem):
    copies = [
        pltpu.make_async_copy(f_hbm, f_ref, sem.at[0]),
        pltpu.make_async_copy(cols_hbm, cols_ref, sem.at[1]),
    ]
    for copy in copies:
        copy.start()
    for copy in copies:
        copy.wait()


def stage1_kernel(bent, cols_ref, f_ref, top_hbm, bottom_hbm, inner_hbm, outer_hbm, *refs):
    *halves, first_ref, second_ref, ext, sem = refs
    rows, bs = f_ref.shape[0], f_ref.shape[2]
    half = first_ref.shape[1]
    row_idx, col_idx = lax.axis_index("row"), lax.axis_index("col")
    base = row_idx * rows
    halo, part = inner_hbm.shape[0], top_hbm.shape[0]
    below = halo + 2 * part
    odd = lax.rem(row_idx, 2)
    inner_at = pl.multiple_of((1 - odd) * below, bs)
    outer_at = pl.multiple_of(odd * below, bs)

    def copies(at, pieces, sems):
        for piece, n in zip(pieces, sems):
            yield pltpu.make_async_copy(piece, ext.at[pl.ds(at, piece.shape[0])], sem.at[n])
            at += piece.shape[0]

    def all_copies(act):
        for copy in copies(halo, (top_hbm, bottom_hbm), (0, 1)):
            act(copy)
        for copy in copies(inner_at, (inner_hbm,), (2,)):
            act(copy)
        if not halves:
            for copy in copies(outer_at, (outer_hbm,), (3,)):
                act(copy)
            return
        is_bent = (row_idx == bent[0]) | (row_idx == bent[1])

        @pl.when(jnp.logical_not(is_bent))
        def _():
            for copy in copies(outer_at, (outer_hbm,), (3,)):
                act(copy)

        @pl.when(is_bent)
        def _():
            for copy in copies(outer_at, halves, (3, 4)):
                act(copy)

    all_copies(lambda copy: copy.start())
    all_copies(lambda copy: copy.wait())
    tile = min(256, half)
    odd = lax.rem(col_idx, 2)
    for i in range(rows):
        lhs = jnp.concatenate([f_ref[i, e] for e in range(STENCIL)], axis=1)
        starts = [
            pl.multiple_of((cols_ref[e, base + i] - base + BAND) * bs, bs)
            for e in range(STENCIL)
        ]
        for part, out_ref in ((1 - odd, first_ref), (odd, second_ref)):
            for t in range(half // tile):
                at = pl.ds(pl.multiple_of(part * half + t * tile, bs), tile)
                rhs = jnp.concatenate([ext[pl.ds(s, bs), at] for s in starts], axis=0)
                out_ref[i * bs : (i + 1) * bs, t * tile : (t + 1) * tile] = jnp.dot(
                    lhs, rhs, preferred_element_type=jnp.float32
                ).astype(out_ref.dtype)


def stage2_kernel(fan, turn, cols_ref, mask_ref, q_ref, w_ref, f_ref, *refs):
    ready = []
    if turn == 0:
        *parts, made, ext, sem = refs
    else:
        ext, *ready = refs[:-4] if turn == fan - 1 else refs[:-1]
        parts = []
        if turn == fan - 1:
            out_hbm, made, out_sem, ready_sem = refs[-4:]
        else:
            made = refs[-1]
    group, bs = f_ref.shape[0], f_ref.shape[2]
    rows, slab = mask_ref.shape
    row_idx, col_idx = lax.axis_index("row"), lax.axis_index("col")
    first = col_idx * slab - BAND

    def column(turn, n):
        return lax.rem(row_idx + turn, fan) * group + n

    def place(j):
        return pl.ds(pl.multiple_of(j * bs, bs), bs)

    stores = []
    for before, done in enumerate(ready):
        for n in range(group):
            to = out_hbm.at[:, place(column(before, n))]
            stores.append(pltpu.make_async_copy(done.at[n], to, ready_sem.at[before, n]))
    joins = []
    odd = lax.rem(col_idx, 2)
    for piece, part in enumerate(parts):
        width = part.shape[1]
        at = odd * piece + (1 - odd) * (len(parts) - 1 - piece)
        to = ext.at[:, pl.ds(pl.multiple_of(at * width, width), width)]
        joins.append(pltpu.make_async_copy(part, to, sem.at[piece]))
    for copy in joins + stores:
        copy.start()
    for copy in joins:
        copy.wait()

    eye = lax.broadcasted_iota(jnp.int32, (bs, bs), 0) == lax.broadcasted_iota(
        jnp.int32, (bs, bs), 1
    )
    for n in range(group):
        j = column(turn, n)
        col = col_idx * slab + j
        to = place(j)
        lhs = jnp.concatenate(
            [
                ext[:, pl.ds(pl.multiple_of((cols_ref[e, col] - first) * bs, bs), bs)]
                for e in range(STENCIL)
            ],
            axis=1,
        )
        rhs = jnp.concatenate([f_ref[n, e] for e in range(STENCIL)], axis=1)
        spread = lax.dot_general(
            lhs, rhs, (((1,), (1,)), ((), ())), preferred_element_type=jnp.float32
        )
        for i in range(rows):
            at = slice(i * bs, (i + 1) * bs)
            keep = mask_ref[i, j].astype(jnp.float32)
            on_main = (row_idx * rows + i == col).astype(jnp.float32)
            noise = jnp.where(eye, q_ref[i : i + 1, :] * on_main, 0.0)
            made[n, at, :] = w_ref[at, to].astype(jnp.float32) * (spread[at] * keep) + noise
        if turn == fan - 1:
            store = pltpu.make_async_copy(made.at[n], out_hbm.at[:, to], out_sem.at[n])
            store.start()
            stores.append(store)
    for store in stores:
        store.wait()


def forecast(
    p_cov, f_blocks, stencil_cols, localization_weights, block_mask, disturbance_variances
):
    rows, cols = lax.axis_size("row"), lax.axis_size("col")
    fan = rows // cols
    block_rows, bs = f_blocks.shape[0], f_blocks.shape[2]
    tall, wide = p_cov.shape
    slab = wide // bs
    halo = BAND * bs
    assert tall == halo and wide == 2 * halo
    cols_of = stencil_cols.T

    smem = pl.BlockSpec(memory_space=pltpu.SMEM)
    hbm = pl.BlockSpec(memory_space=ANY)
    vmem = pl.BlockSpec(memory_space=pltpu.VMEM)
    top, bottom = p_cov[: tall // 2], p_cov[tall // 2 :]
    f_near, cols_of = pl.pallas_call(
        fetch_kernel,
        out_shape=tuple(jax.ShapeDtypeStruct(x.shape, x.dtype) for x in (f_blocks, cols_of)),
        in_specs=[hbm, hbm],
        out_specs=(vmem, vmem),
        scratch_shapes=[pltpu.SemaphoreType.DMA((2,))],
        compiler_params=pltpu.CompilerParams(vmem_limit_bytes=8 * 2**20),
        name="fetch",
    )(f_blocks, cols_of)

    inner_pairs, outer_pairs = exchanges(rows)
    bent, halves = (rows // 2, rows // 2 - 1), ()
    if (cols, fan) == (4, 2):
        lower, upper = bent
        across = [(upper, lower), (lower, upper)]
        outer_pairs = [pair for pair in outer_pairs if pair not in across]
        straight = lax.ppermute(top, "row", across)
        turn = lax.ppermute(bottom, "row", [(upper, rows - 1), (lower, 0)])
        turned = lax.ppermute(turn, "row", [(rows - 1, lower), (0, upper)])
        halves = (straight, turned)
    inner = lax.ppermute(p_cov, "row", inner_pairs)
    outer = lax.ppermute(p_cov, "row", outer_pairs)
    held = [f_blocks]
    for source, pairs in group_plan(rows, cols):
        busy = {i for pair in pairs for i in pair}
        idle = [(i, i) for i in range(rows * cols) if i not in busy]
        held.append(lax.ppermute(held[source], ("row", "col"), pairs + idle))

    half = jax.ShapeDtypeStruct((tall, halo), jnp.bfloat16)
    first, second = pl.pallas_call(
        functools.partial(stage1_kernel, bent),
        out_shape=(half, half),
        in_specs=[smem, vmem] + [hbm] * (4 + len(halves)),
        out_specs=(vmem, vmem),
        scratch_shapes=[
            pltpu.VMEM((tall + 2 * halo, wide), jnp.bfloat16),
            pltpu.SemaphoreType.DMA((5,)),
        ],
        compiler_params=pltpu.CompilerParams(vmem_limit_bytes=16 * 2**20),
        name="stage1",
    )(cols_of, f_near, top, bottom, inner, outer, *halves)

    inner_pairs, outer_pairs = exchanges(cols)
    idle = set(range(cols)) - {i for i, _ in outer_pairs}
    outer_pairs = outer_pairs + [(i, i) for i in sorted(idle)]
    nearer = lax.ppermute(first, "col", inner_pairs)
    further = lax.ppermute(second, "col", outer_pairs)

    mine = pl.pallas_call(
        functools.partial(pick_kernel, holder_table(rows, cols)),
        out_shape=jax.ShapeDtypeStruct(f_blocks.shape, f_blocks.dtype),
        in_specs=[hbm] * len(held),
        out_specs=vmem,
        scratch_shapes=[pltpu.SemaphoreType.DMA((block_rows,))],
        compiler_params=pltpu.CompilerParams(vmem_limit_bytes=4 * 2**20),
        name="pick",
    )(*held)
    fixed = (
        cols_of,
        block_mask,
        disturbance_variances.reshape(block_rows, bs),
        localization_weights,
    )
    assert fan > 1
    group = slab // fan
    made_type = jax.ShapeDtypeStruct((group, tall, bs), jnp.float32)
    params = pltpu.CompilerParams(vmem_limit_bytes=20 * 2**20)
    made, ext = pl.pallas_call(
        functools.partial(stage2_kernel, fan, 0),
        out_shape=(made_type, jax.ShapeDtypeStruct((tall, wide + 2 * halo), jnp.bfloat16)),
        in_specs=[smem, smem, vmem, vmem, vmem] + [hbm] * 4,
        out_specs=(vmem, vmem),
        scratch_shapes=[pltpu.SemaphoreType.DMA((4,))],
        compiler_params=params,
        name="stage2",
    )(*fixed, mine, nearer, first, second, further)
    ready = [made]
    for turn in range(1, fan):
        last = turn == fan - 1
        pairs = [(r // fan * fan + (r + turn) % fan, r) for r in range(rows)]
        other = lax.ppermute(mine, "row", pairs)
        ready.append(
            pl.pallas_call(
                functools.partial(stage2_kernel, fan, turn),
                out_shape=jax.ShapeDtypeStruct((tall, wide), jnp.float32) if last else made_type,
                in_specs=[smem, smem, vmem, vmem, vmem, vmem] + [vmem] * (len(ready) * last),
                out_specs=pl.BlockSpec(memory_space=pltpu.HBM) if last else vmem,
                scratch_shapes=[
                    pltpu.VMEM(made_type.shape, made_type.dtype),
                    pltpu.SemaphoreType.DMA((group,)),
                    pltpu.SemaphoreType.DMA((turn, group)),
                ]
                * last,
                compiler_params=params,
                name="stage3",
            )(*fixed, other, ext, *(ready * last))
        )
    return ready[-1]


def solution(mesh):
    placed = (
        P("row", "col"),
        P("row", None, None, None),
        P(),
        P("row", "col"),
        P("row", "col"),
        P("row"),
    )
    return jax.shard_map(
        forecast, mesh=mesh, in_specs=placed, out_specs=P("row", "col"), check_vma=False
    )
```
